256 devices in a mesh: seq: 32 (over x, z), head: 8 (over y, core).
Axes of the slice: x: 4, y: 4, z: 8, core: 2. Of those that a mesh axis runs over, the one named last changes fastest.
Arguments:
- queries: bfloat16 [8192, 4096], P('seq', 'head'), may hold values from -8 to 8
- suffix_key_value: bfloat16 [8192, 2, 2048], P('seq', None, 'head'), may hold values from -8 to 8
- pooled_pages: bfloat16 [512, 256, 2, 2048], P('seq', None, None, 'head'), may hold values from -8 to 8
- out_weight: bfloat16 [4096, 5376], P('head'), may hold values from -0.5 to 0.5
- page_table: int32 [16, 32], replicated, may hold values from 0 to 511, as said below
- prefix_len: int32 [16], replicated, may hold values from 1024 to 8192, as said below
- suffix_len: int32 [16], replicated, may hold values from 2 to 512, as said below
Outputs:
- projected: bfloat16 [8192, 5376], P('seq', 'head')
The draws below stay inside these ranges and needn't reach their ends.
Inputs may be any that keep to these rules, and one draw needn't show every extreme that they name: `page_table`: every slot of the pool appears exactly once; slot s lies on index s // 16 of seq, and every index of seq holds exactly 1 pages of every request. `prefix_len`: some request has exactly 8192 prefix tokens. `suffix_len`: some request has exactly 512 live suffix tokens.
All inputs are finite; a program needn't handle non-finite values.
Results may differ from the reference program's by a relative error of at most 0.013.
Values may be sent and summed in bfloat16 or wider, within the bound.
A program may use at most 128 MiB of HBM per device.

```python
import jax
import jax.numpy as jnp
from jax import lax

D = 5376
QUERY_HEADS = 32
KEY_VALUE_HEADS = 16
HEAD_WIDTH = 128
PAGE_TOKENS = 256
TOK_DEV = 256
PAGES_DEV = 16
SUFFIX_TOKENS = 512
REQUEST_COUNT = 16
PREFIX_PAGES = 32
CAP = 1
POOL_PAGES = 512
TOTAL_TOKENS = 8192
N_HEAD = 8


def draw_queries(key, part):
    unsigned_values = jnp.clip(2.0 * jax.random.normal(jax.random.fold_in(key, 32), (TOTAL_TOKENS, QUERY_HEADS * HEAD_WIDTH), jnp.float32), -8.0, 8.0)
    return unsigned_values.astype(jnp.bfloat16)


def draw_suffix_key_value(key, part):
    unsigned_values = jnp.clip(jax.random.normal(jax.random.fold_in(key, 33), (TOTAL_TOKENS, 2, KEY_VALUE_HEADS * HEAD_WIDTH), jnp.float32), -8.0, 8.0)
    return unsigned_values.astype(jnp.bfloat16)


def shuffle_local(subkey):
    return jax.random.permutation(subkey, PAGES_DEV)


def shuffle_pages(subkey):
    return jax.random.permutation(subkey, PREFIX_PAGES)


def draw_page_table(key, part):
    device_count = POOL_PAGES // PAGES_DEV
    local_order = jax.vmap(shuffle_local)(jax.random.split(jax.random.fold_in(key, 11), device_count))
    page_order = jax.vmap(shuffle_pages)(jax.random.split(jax.random.fold_in(key, 12), REQUEST_COUNT))
    device_of = page_order // CAP
    within = page_order % CAP
    request_ids = jnp.arange(REQUEST_COUNT, dtype=jnp.int32)[:, None]
    local_slot = local_order[device_of, request_ids * CAP + within]
    return (device_of * PAGES_DEV + local_slot).astype(jnp.int32)


def draw_prefix_len(key, part):
    longest = PREFIX_PAGES * PAGE_TOKENS
    floor_len = longest // 8
    first_draw = jax.random.randint(jax.random.fold_in(key, 21), (REQUEST_COUNT,), 0, longest - floor_len + 1)
    second = jax.random.randint(jax.random.fold_in(key, 22), (REQUEST_COUNT,), 0, longest - floor_len + 1)
    lengths = floor_len + jnp.minimum(first_draw, second)
    chosen = jax.random.randint(jax.random.fold_in(key, 23), (), 0, REQUEST_COUNT)
    return jnp.where(jnp.arange(REQUEST_COUNT, dtype=jnp.int32) == chosen, longest, lengths).astype(jnp.int32)


def draw_suffix_len(key, part):
    lengths = jax.random.randint(jax.random.fold_in(key, 24), (REQUEST_COUNT,), 2, SUFFIX_TOKENS + 1)
    chosen = jax.random.randint(jax.random.fold_in(key, 25), (), 0, REQUEST_COUNT)
    return jnp.where(jnp.arange(REQUEST_COUNT, dtype=jnp.int32) == chosen, SUFFIX_TOKENS, lengths).astype(jnp.int32)


def steps_of(own_key, dims, shards, least, high):
    gain = 1.0
    for dim, blocks in shards:
        heights = jax.random.uniform(jax.random.fold_in(jax.random.fold_in(own_key, 6), dim), (blocks,), jnp.float32, least / len(shards), high / len(shards))
        gain = gain * jnp.repeat(jnp.exp(heights), dims[dim] // blocks).reshape((-1,) + (1,) * (len(dims) - 1 - dim))
    return gain


def gaussian(key, extent, deviation, bound, cuts=(), held_as=jnp.bfloat16):
    entries = jax.random.normal(key, extent, jnp.float32) * deviation
    if len(cuts) > 0:
        entries = steps_of(key, extent, cuts, -0.22, 0.18) * entries
    return jnp.clip(entries, min=-bound, max=bound).astype(held_as)


def setup_inputs(seed: int = 0) -> dict:
    key_of = jax.random.split(jax.random.key(seed), 8)
    queries = draw_queries(jax.random.fold_in(key_of[7], 71), 0)
    suffix_key_value = draw_suffix_key_value(jax.random.fold_in(key_of[7], 71), 0)
    pooled_pages = gaussian(key_of[2], (POOL_PAGES, PAGE_TOKENS, 2, KEY_VALUE_HEADS * HEAD_WIDTH), 1.0, 8.0, ((0, 32), (3, 8)))
    out_weight = gaussian(key_of[3], (QUERY_HEADS * HEAD_WIDTH, D), HEAD_WIDTH ** -0.5, 0.5, ((0, 8),))
    page_table = draw_page_table(jax.random.fold_in(key_of[7], 71), 0)
    prefix_len = draw_prefix_len(jax.random.fold_in(key_of[7], 71), 0)
    suffix_len = draw_suffix_len(jax.random.fold_in(key_of[7], 71), 0)
    return dict(queries=queries, suffix_key_value=suffix_key_value, pooled_pages=pooled_pages, out_weight=out_weight, page_table=page_table, prefix_len=prefix_len, suffix_len=suffix_len)


def reference(queries, suffix_key_value, pooled_pages, out_weight, page_table, prefix_len, suffix_len):
    group_of_heads = QUERY_HEADS // KEY_VALUE_HEADS
    score_scale = float(D // QUERY_HEADS) ** -0.5
    query_layout = jnp.swapaxes(queries.reshape(2, REQUEST_COUNT, TOK_DEV, KEY_VALUE_HEADS, group_of_heads, HEAD_WIDTH), 0, 1).reshape(REQUEST_COUNT, SUFFIX_TOKENS, KEY_VALUE_HEADS, group_of_heads, HEAD_WIDTH)
    suffix_layout = jnp.swapaxes(suffix_key_value.reshape(2, REQUEST_COUNT, TOK_DEV, 2, KEY_VALUE_HEADS, HEAD_WIDTH), 0, 1).reshape(REQUEST_COUNT, SUFFIX_TOKENS, 2, KEY_VALUE_HEADS, HEAD_WIDTH)
    positions = jnp.arange(SUFFIX_TOKENS, dtype=jnp.int32)
    prefix_positions = jnp.arange(PREFIX_PAGES * PAGE_TOKENS, dtype=jnp.int32)

    def one_request(inputs):
        query_req, suffix_req, page_table_row, prefix_count, suffix_count = inputs
        rows_of_pages = jnp.take(pooled_pages, page_table_row.astype(jnp.int32), axis=0).reshape(PREFIX_PAGES * PAGE_TOKENS, 2, KEY_VALUE_HEADS, HEAD_WIDTH)
        key_rows = jnp.concatenate([rows_of_pages[:, 0], suffix_req[:, 0]], axis=0)
        value_rows = jnp.concatenate([rows_of_pages[:, 1], suffix_req[:, 1]], axis=0)
        prefix_seen = jnp.broadcast_to((prefix_positions < prefix_count)[None, :], (SUFFIX_TOKENS, PREFIX_PAGES * PAGE_TOKENS))
        suffix_seen = (positions[None, :] <= positions[:, None]) & (positions[None, :] < suffix_count)
        visible = jnp.concatenate([prefix_seen, suffix_seen], axis=1)
        live_query = positions < suffix_count

        def one_head(head_inputs):
            query_head, key_head, value_head = head_inputs
            scores = jnp.einsum("tgd,nd->tgn", query_head.astype(jnp.float32), key_head.astype(jnp.float32)) * score_scale
            row_max = jnp.max(jnp.where(visible[:, None, :], scores, -jnp.inf), axis=2, keepdims=True)
            weights = jnp.where(visible[:, None, :], jnp.exp(scores - row_max), 0.0)
            row_total = jnp.sum(weights, axis=2, keepdims=True)
            rounded = lax.optimization_barrier(weights.astype(jnp.bfloat16)).astype(jnp.float32)
            mixed = jnp.einsum("tgn,nd->tgd", rounded, value_head.astype(jnp.float32)) / row_total
            return jnp.where(live_query[:, None, None], mixed, 0.0).astype(jnp.bfloat16)

        head_outs = lax.map(one_head, (jnp.moveaxis(query_req, 1, 0), jnp.moveaxis(key_rows, 1, 0), jnp.moveaxis(value_rows, 1, 0)))
        return jnp.moveaxis(head_outs, 0, 1).reshape(SUFFIX_TOKENS, QUERY_HEADS * HEAD_WIDTH)

    attention = lax.map(one_request, (query_layout, suffix_layout, page_table, prefix_len, suffix_len))
    attention = jnp.swapaxes(attention.reshape(REQUEST_COUNT, 2, TOK_DEV, QUERY_HEADS * HEAD_WIDTH), 0, 1)
    attention = attention.reshape(REQUEST_COUNT * SUFFIX_TOKENS, QUERY_HEADS * HEAD_WIDTH)
    group_cols = QUERY_HEADS * HEAD_WIDTH // N_HEAD
    projected = jnp.zeros((REQUEST_COUNT * SUFFIX_TOKENS, D), jnp.float32)
    for head_slot in range(N_HEAD):
        partial_value = jnp.dot(attention[:, head_slot * group_cols:(head_slot + 1) * group_cols], out_weight[head_slot * group_cols:(head_slot + 1) * group_cols], preferred_element_type=jnp.float32)
        projected = projected + lax.optimization_barrier(partial_value.astype(jnp.bfloat16)).astype(jnp.float32)
    return projected.astype(jnp.bfloat16)
```

```python
import functools

import jax
import jax.numpy as jnp
from jax import lax
from jax.experimental import pallas as pl
from jax.experimental.pallas import tpu as pltpu
from jax.sharding import PartitionSpec as P

D = 5376
QUERY_HEADS = 32
KEY_VALUE_HEADS = 16
HEAD_WIDTH = 128
NX, NZ, NY = 4, 8, 4
ROWS = 256
PAGES = 16
NEG = -1e30
SCALE2 = float(D // QUERY_HEADS) ** (-0.5) * 1.4426950408889634
CHIP_COLS = D // NY
WIDE = 1408
DEV_COLS = D // 8
MESH = pl.DeviceIdType.MESH

MESSAGES = (
    ("h", 0, 0), ("h", 1, 0), ("h", 0, 1),
    ("s", 0, 0), ("s", 1, 0), ("s", 3, 0), ("s", 2, 0), ("s", 0, 1),
    ("h", 0, -1), ("h", 1, 1), ("h", 1, -1),
    ("s", 1, 1), ("s", 3, 1), ("s", 0, 2), ("s", 2, 1), ("s", 3, 2),
)
SELF = (0, 3)


def sign(x):
    return 1 - 2 * (x // 2)


def wrap(v, n):
    return lax.rem(v + 4 * n, n)


def home_step(j, dz):
    if j == 0:
        return 0, -dz
    return (-1, 0) if dz == 0 else (1, -dz)


def dest_of(message, x, z):
    kind, a, b = message
    if kind == "h":
        dx, dz = home_step(a, b)
        return wrap(x + dx, NX), wrap(z + dz, NZ)
    to = wrap(x + a, NX)
    return to, wrap(z - sign(to) * b, NZ)


def source_of(message, x, z):
    kind, a, b = message
    if kind == "h":
        dx, dz = home_step(a, b)
        return wrap(x - dx, NX), wrap(z - dz, NZ)
    return wrap(x - a, NX), wrap(z + sign(x) * b, NZ)


def request_of(message, x, z):
    if message[0] == "h":
        return lax.rem(x, 2) * NZ + z
    return lax.rem(x, 2) * NZ + wrap(z - 2 * sign(x), NZ)


def kernel(
    table, suffix_len, q_hbm, skv_hbm, pages_hbm, w_hbm, out_ref,
    pages, sending, kv, skv, q_all, w_all, acc, m_ref, l_ref,
    o_out, o_in, st_out, st_in, attn, total, sib_out, sib_in,
    local_sem, q_send, q_recv, p_send, p_recv, w_send, w_recv,
    o_send, o_recv, t_send, t_recv, a_send, a_recv, b_send, b_recv,
):
    seq = lax.axis_index("seq")
    head = lax.axis_index("head")
    x, z = seq // NZ, lax.rem(seq, NZ)
    y, core = head // 2, lax.rem(head, 2)
    s = sign(x)

    def node(xx, zz):
        return {"seq": xx * NZ + zz, "head": head}

    def chip(dy):
        return {"seq": seq, "head": wrap(y + dy, NY) * 2 + core}

    sibling = {"seq": seq, "head": y * 2 + 1 - core}
    partner = node(wrap(x + 2, NX), z)
    side_near = (x, wrap(z + 2 * s, NZ))
    side_far = (wrap(x + 2, NX), wrap(z - 2 * s, NZ))
    own_side_near = (x, wrap(z - 2 * s, NZ))

    local = [
        pltpu.make_async_copy(pages_hbm, pages, local_sem.at[0]),
        pltpu.make_async_copy(q_hbm, q_all.at[0, 0], local_sem.at[1]),
        pltpu.make_async_copy(skv_hbm, skv, local_sem.at[2]),
    ]
    for copy in local:
        copy.start()

    barrier = pltpu.get_barrier_semaphore()
    heard = 0
    for k, message in enumerate(MESSAGES):
        if k in SELF:
            continue
        pl.semaphore_signal(
            barrier, inc=1, device_id=node(*source_of(message, x, z)), device_id_type=MESH
        )
        heard += 1
    for where in (own_side_near, side_far):
        pl.semaphore_signal(barrier, inc=1, device_id=node(*where), device_id_type=MESH)
        heard += 1
    for dy in (1, 2, 3):
        pl.semaphore_signal(barrier, inc=1, device_id=chip(dy), device_id_type=MESH)
        heard += 1
    pl.semaphore_signal(barrier, inc=1, device_id=sibling, device_id_type=MESH)
    heard += 1

    acc[...] = jnp.zeros_like(acc)
    m_ref[...] = jnp.full(m_ref.shape, NEG, jnp.float32)
    l_ref[...] = jnp.zeros_like(l_ref)
    local[0].wait()
    for k in range(PAGES):
        buffer = kv if k in SELF else sending
        buffer[k] = pages[table[k]]
    pl.semaphore_wait(barrier, heard)

    def remote(src, dst, send, recv, to):
        return pltpu.make_async_remote_copy(
            src_ref=src, dst_ref=dst, send_sem=send, recv_sem=recv,
            device_id=to, device_id_type=MESH,
        )

    q_copies = [
        remote(q_hbm, q_all.at[0, 1], q_send.at[0], q_recv.at[0], partner),
        remote(q_hbm, q_all.at[1, 0], q_send.at[1], q_recv.at[1], node(*side_near)),
        remote(q_hbm, q_all.at[1, 1], q_send.at[2], q_recv.at[2], node(*side_far)),
    ]
    for copy in q_copies:
        copy.start()

    def column(of):
        return pl.multiple_of(((21 * of) // 2) * 128, 128)

    own_weight = pltpu.make_async_copy(
        w_hbm.at[:, pl.ds(column(y), WIDE)], w_all.at[y], local_sem.at[3]
    )
    own_weight.start()
    w_copies = []
    for dy in (1, 3, 2):
        of = wrap(y + dy, NY)
        w_copies.append(
            remote(
                w_hbm.at[:, pl.ds(column(of), WIDE)], w_all.at[y],
                w_send.at[dy - 1], w_recv.at[dy - 1], chip(dy),
            )
        )
        w_copies[-1].start()

    p_copies = []
    for k, message in enumerate(MESSAGES):
        if k in SELF:
            continue
        copy = remote(
            sending.at[k], kv.at[k], p_send.at[k], p_recv.at[k],
            node(*dest_of(message, x, z)),
        )
        copy.start()
        p_copies.append(copy)

    rows = lax.broadcasted_iota(jnp.int32, (ROWS, ROWS), 0)
    cols = lax.broadcasted_iota(jnp.int32, (ROWS, ROWS), 1)

    def attend(st, block, masks, members=(0, 1)):
        for g in range(2):
            lanes = slice(g * HEAD_WIDTH, (g + 1) * HEAD_WIDTH)
            keys = block[:, 0, lanes]
            values = block[:, 1, lanes].T
            for mi in members:
                for u in range(2):
                    first = (2 * g + u) * HEAD_WIDTH
                    query = q_all[st, mi, :, first:first + HEAD_WIDTH]
                    c = (g * 2 + mi) * 2 + u
                    scores = lax.dot_general(
                        keys, query, (((1,), (1,)), ((), ())),
                        preferred_element_type=jnp.float32,
                    )
                    scores = jnp.where(masks[mi], scores, NEG)
                    old = m_ref[st, c:c + 1, :]
                    new = jnp.maximum(old, jnp.max(scores, axis=0, keepdims=True))
                    weights = jnp.exp2((scores - new) * SCALE2)
                    keep = jnp.exp2((old - new) * SCALE2)
                    m_ref[st, c:c + 1, :] = new
                    l_ref[st, c:c + 1, :] = l_ref[st, c:c + 1, :] * keep + jnp.sum(
                        weights, axis=0, keepdims=True
                    )
                    mixed = jnp.dot(
                        values, weights.astype(jnp.bfloat16),
                        preferred_element_type=jnp.float32,
                    )
                    acc[st, c] = acc[st, c] * keep + mixed

    member = x // 2
    mine = suffix_len[lax.rem(x, 2) * NZ + z]
    here = mine - member * ROWS
    local[1].wait()
    local[2].wait()
    q_copies[0].wait_recv()
    attend(
        0, skv,
        {0: (rows <= cols) & (rows < here), 1: rows < here * (1 - member)},
    )
    q_copies[1].wait_recv()
    q_copies[2].wait_recv()

    def step(i, carry):
        st = (lax.rem(i, 8) + 5) // 8

        @pl.when((i != SELF[0]) & (i != SELF[1]))
        def _():
            remote(
                sending.at[i], kv.at[i], p_send.at[i], p_recv.at[i], partner
            ).wait_recv()

        mask = rows < table[PAGES + i]
        attend(st, kv.at[i], {0: mask, 1: mask})
        return carry

    lax.fori_loop(0, PAGES, step, 0)

    targets = ((0, 1, partner), (1, 0, node(*own_side_near)), (1, 1, node(*side_far)))
    o_copies = {}
    for g in range(2):
        for n, (st, mi, to) in enumerate(targets):
            for u in range(2):
                c = (g * 2 + mi) * 2 + u
                share = l_ref[st, c:c + 1, :]
                o_out[g, n, u] = (acc[st, c] / share).astype(jnp.bfloat16)
                st_out[g, n, u:u + 1, :] = m_ref[st, c:c + 1, :]
                st_out[g, n, 2 + u:3 + u, :] = share
            e = g * 3 + n
            pair = (
                remote(st_out.at[g, n], st_in.at[g, n], t_send.at[e], t_recv.at[e], to),
                remote(o_out.at[g, n], o_in.at[g, n], o_send.at[e], o_recv.at[e], to),
            )
            for copy in pair:
                copy.start()
            o_copies[g, n] = pair

    a_copies = {}
    live = lax.broadcasted_iota(jnp.int32, (1, ROWS), 1) < here
    for g in range(2):
        for n in range(3):
            for copy in o_copies[g, n]:
                copy.wait_recv()
        for u in range(2):
            c = g * 4 + u
            tops = [m_ref[0, c:c + 1, :]] + [st_in[g, n, u:u + 1, :] for n in range(3)]
            sums = [l_ref[0, c:c + 1, :]] + [st_in[g, n, 2 + u:3 + u, :] for n in range(3)]
            top = jnp.maximum(jnp.maximum(tops[0], tops[1]), jnp.maximum(tops[2], tops[3]))
            factors = [jnp.exp2((t - top) * SCALE2) for t in tops]
            shares = [f * l for f, l in zip(factors, sums)]
            whole = shares[0] + shares[1] + shares[2] + shares[3]
            inverse = jnp.where(live, 1.0 / whole, 0.0)
            value = acc[0, c] * (factors[0] * inverse)
            for n in range(3):
                value += o_in[g, n, u].astype(jnp.float32) * (shares[n + 1] * inverse)
            first = (2 * g + u) * HEAD_WIDTH
            attn[y, :, first:first + HEAD_WIDTH] = value.T.astype(jnp.bfloat16)
        half = pl.ds(g * 256, 256)
        for dy in (1, 3, 2):
            e = g * 3 + dy - 1
            copy = remote(
                attn.at[y, :, half], attn.at[y, :, half], a_send.at[e], a_recv.at[e], chip(dy)
            )
            copy.start()
            a_copies[g, dy] = copy

    own_weight.wait()
    total[...] = jnp.dot(attn[y], w_all[y], preferred_element_type=jnp.float32)
    for n, dy in enumerate((1, 3, 2)):
        w_copies[n].wait_recv()
    for g in range(2):
        for dy in (1, 3, 2):
            a_copies[g, dy].wait_recv()
            of = wrap(y - dy, NY)
            total[...] += jnp.dot(
                attn[of, :, g * 256:(g + 1) * 256], w_all[of, g * 256:(g + 1) * 256, :],
                preferred_element_type=jnp.float32,
            )

    def columns_of(c):
        return pltpu.roll(total[...], WIDE - 64 * lax.rem(y, 2) - DEV_COLS * c, 1)[:, :768]

    sib_out[...] = columns_of(1 - core).astype(jnp.bfloat16)
    swap = remote(sib_out, sib_in, b_send.at[0], b_recv.at[0], sibling)
    swap.start()
    own = columns_of(core)
    swap.wait_recv()
    out_ref[...] = (own + sib_in[...].astype(jnp.float32)).astype(jnp.bfloat16)[:, :DEV_COLS]

    for copy in q_copies + w_copies + p_copies + list(a_copies.values()) + [swap]:
        copy.wait_send()
    for pair in o_copies.values():
        for copy in pair:
            copy.wait_send()


def shards(queries, suffix_key_value, pooled_pages, out_weight, page_table, prefix_len, suffix_len):
    seq = lax.axis_index("seq")
    x, z = seq // NZ, lax.rem(seq, NZ)
    devices, requests = [], []
    for message in MESSAGES:
        devices.append(seq)
        requests.append(request_of(message, *dest_of(message, x, z)))
    for message in MESSAGES:
        xx, zz = source_of(message, x, z)
        devices.append(xx * NZ + zz)
        requests.append(request_of(message, x, z))
    devices = jnp.stack(devices)[:, None, None]
    requests = jnp.stack(requests)[:, None, None]
    request = jnp.arange(page_table.shape[0], dtype=jnp.int32)[None, :, None]
    position = jnp.arange(page_table.shape[1], dtype=jnp.int32)[None, None, :] * ROWS
    entry = jnp.arange(2 * PAGES, dtype=jnp.int32)[:, None, None]
    chosen = (request == requests) & (page_table[None] // PAGES == devices)
    value = jnp.where(
        entry < PAGES, page_table[None] % PAGES, prefix_len[None, :, None] - position
    )
    table = jnp.sum(jnp.where(chosen, value, 0), axis=(1, 2))

    vmem = pltpu.VMEM
    dma = pltpu.SemaphoreType.DMA
    bf16, f32 = jnp.bfloat16, jnp.float32
    return pl.pallas_call(
        kernel,
        out_shape=jax.ShapeDtypeStruct((ROWS, DEV_COLS), bf16),
        in_specs=[pl.BlockSpec(memory_space=pltpu.SMEM)] * 2
        + [pl.BlockSpec(memory_space=pl.ANY)] * 4,
        out_specs=pl.BlockSpec(memory_space=vmem),
        scratch_shapes=[
            vmem((PAGES, ROWS, 2, 256), bf16),
            vmem((PAGES, ROWS, 2, 256), bf16),
            vmem((PAGES, ROWS, 2, 256), bf16),
            vmem((ROWS, 2, 256), bf16),
            vmem((2, 2, ROWS, 512), bf16),
            vmem((NY, 512, WIDE), bf16),
            vmem((2, 8, HEAD_WIDTH, ROWS), f32),
            vmem((2, 8, ROWS), f32),
            vmem((2, 8, ROWS), f32),
            vmem((2, 3, 2, HEAD_WIDTH, ROWS), bf16),
            vmem((2, 3, 2, HEAD_WIDTH, ROWS), bf16),
            vmem((2, 3, 8, ROWS), f32),
            vmem((2, 3, 8, ROWS), f32),
            vmem((NY, ROWS, 512), bf16),
            vmem((ROWS, WIDE), f32),
            vmem((ROWS, 768), bf16),
            vmem((ROWS, 768), bf16),
            dma((4,)), dma((3,)), dma((3,)), dma((PAGES,)), dma((PAGES,)), dma((3,)), dma((3,)),
            dma((6,)), dma((6,)), dma((6,)), dma((6,)), dma((6,)), dma((6,)), dma((1,)), dma((1,)),
        ],
        compiler_params=pltpu.CompilerParams(
            collective_id=0, has_side_effects=True, vmem_limit_bytes=56 * 1024 * 1024
        ),
        name="paged_prefill",
    )(table, suffix_len, queries, suffix_key_value, pooled_pages, out_weight)


def solution(mesh):
    placed = (
        P("seq", "head"),
        P("seq", None, "head"),
        P("seq", None, None, "head"),
        P("head", None),
        P(),
        P(),
        P(),
    )
    return jax.shard_map(
        shards, mesh=mesh, in_specs=placed, out_specs=P("seq", "head"), check_vma=False
    )
```

```python
import functools

import jax
import jax.numpy as jnp
from jax import lax
from jax.experimental import pallas as pl
from jax.experimental.pallas import tpu as pltpu
from jax.sharding import PartitionSpec as P

D = 5376
QUERY_HEADS = 32
KEY_VALUE_HEADS = 16
HEAD_WIDTH = 128
NX, NZ, NY = 4, 8, 4
ROWS = 256
PAGES = 16
NEG = -1e30
SCALE2 = float(D // QUERY_HEADS) ** (-0.5) * 1.4426950408889634
CHIP_COLS = D // NY
WIDE = 1408
DEV_COLS = D // 8
MESH = pl.DeviceIdType.MESH

MESSAGES = (
    ("h", 0, 0), ("s", 0, 0),
    ("s", 1, 0), ("s", 3, 0), ("s", 0, 1), ("s", 2, 0), ("s", 0, 2),
    ("s", 1, 1), ("s", 3, 1), ("s", 3, 2), ("s", 2, 1),
    ("h", 0, 1), ("h", 0, -1), ("h", 1, 0), ("h", 1, 1), ("h", 1, -1),
)
SELF = (0, 1)
SIDE_END = 11


def sign(x, z):
    return 1 - 2 * lax.rem(x // 2 + z, 2)


def wrap(v, n):
    return lax.rem(v + 4 * n, n)


def home_step(j, dz):
    if j == 0:
        return 0, -dz
    return (-1, 0) if dz == 0 else (1, -dz)


def dest_of(message, x, z):
    kind, a, b = message
    if kind == "h":
        dx, dz = home_step(a, b)
        return wrap(x + dx, NX), wrap(z + dz, NZ)
    to = wrap(x + a, NX)
    return to, wrap(z - sign(to, z + b) * b, NZ)


def source_of(message, x, z):
    kind, a, b = message
    if kind == "h":
        dx, dz = home_step(a, b)
        return wrap(x - dx, NX), wrap(z - dz, NZ)
    return wrap(x - a, NX), wrap(z + sign(x, z) * b, NZ)


def request_of(message, x, z):
    if message[0] == "h":
        return lax.rem(x, 2) * NZ + z
    return lax.rem(x, 2) * NZ + wrap(z - 2 * sign(x, z), NZ)


def kernel(
    table, suffix_len, q_hbm, skv_hbm, pages_hbm, w_hbm, out_ref,
    pages, sending, kv, skv, q_all, w_all, acc, m_ref, l_ref,
    o_out, o_in, st_out, st_in, attn, total, sib_out, sib_in,
    local_sem, q_send, q_recv, p_send, p_recv, w_send, w_recv,
    o_send, o_recv, t_send, t_recv, a_send, a_recv, b_send, b_recv,
):
    seq = lax.axis_index("seq")
    head = lax.axis_index("head")
    x, z = seq // NZ, lax.rem(seq, NZ)
    y, core = head // 2, lax.rem(head, 2)
    s = sign(x, z)

    def node(xx, zz):
        return {"seq": xx * NZ + zz, "head": head}

    def chip(dy):
        return {"seq": seq, "head": wrap(y + dy, NY) * 2 + core}

    sibling = {"seq": seq, "head": y * 2 + 1 - core}
    partner = node(wrap(x + 2, NX), z)
    side_near = (x, wrap(z + 2 * s, NZ))
    side_far = (wrap(x + 2, NX), wrap(z - 2 * s, NZ))
    own_side_near = (x, wrap(z - 2 * s, NZ))

    local = [
        pltpu.make_async_copy(pages_hbm, pages, local_sem.at[0]),
        pltpu.make_async_copy(q_hbm, q_all.at[0, 0], local_sem.at[1]),
        pltpu.make_async_copy(skv_hbm, skv, local_sem.at[2]),
    ]
    for copy in local:
        copy.start()

    barrier = pltpu.get_barrier_semaphore()
    heard = 0
    for k, message in enumerate(MESSAGES):
        if k in SELF:
            continue
        pl.semaphore_signal(
            barrier, inc=1, device_id=node(*source_of(message, x, z)), device_id_type=MESH
        )
        heard += 1
    for where in (own_side_near, side_far):
        pl.semaphore_signal(barrier, inc=1, device_id=node(*where), device_id_type=MESH)
        heard += 1
    for dy in (1, 2, 3):
        pl.semaphore_signal(barrier, inc=1, device_id=chip(dy), device_id_type=MESH)
        heard += 1
    pl.semaphore_signal(barrier, inc=1, device_id=sibling, device_id_type=MESH)
    heard += 1

    acc[...] = jnp.zeros_like(acc)
    m_ref[...] = jnp.full(m_ref.shape, NEG, jnp.float32)
    l_ref[...] = jnp.zeros_like(l_ref)
    local[0].wait()
    for k in range(PAGES):
        buffer = kv if k in SELF else sending
        buffer[k] = pages[table[k]]
    pl.semaphore_wait(barrier, heard)

    def remote(src, dst, send, recv, to):
        return pltpu.make_async_remote_copy(
            src_ref=src, dst_ref=dst, send_sem=send, recv_sem=recv,
            device_id=to, device_id_type=MESH,
        )

    q_copies = [
        remote(q_hbm, q_all.at[0, 1], q_send.at[0], q_recv.at[0], partner),
        remote(q_hbm, q_all.at[1, 0], q_send.at[1], q_recv.at[1], node(*side_near)),
        remote(q_hbm, q_all.at[1, 1], q_send.at[2], q_recv.at[2], node(*side_far)),
    ]
    for copy in q_copies:
        copy.start()

    def column(of):
        return pl.multiple_of(((21 * of) // 2) * 128, 128)

    own_weight = pltpu.make_async_copy(
        w_hbm.at[:, pl.ds(column(y), WIDE)], w_all.at[y], local_sem.at[3]
    )
    own_weight.start()
    w_copies = []
    for dy in (1, 3, 2):
        of = wrap(y + dy, NY)
        w_copies.append(
            remote(
                w_hbm.at[:, pl.ds(column(of), WIDE)], w_all.at[y],
                w_send.at[dy - 1], w_recv.at[dy - 1], chip(dy),
            )
        )
        w_copies[-1].start()

    p_copies = []
    for k, message in enumerate(MESSAGES):
        if k in SELF:
            continue
        copy = remote(
            sending.at[k], kv.at[k], p_send.at[k], p_recv.at[k],
            node(*dest_of(message, x, z)),
        )
        copy.start()
        p_copies.append(copy)

    rows = lax.broadcasted_iota(jnp.int32, (ROWS, ROWS), 0)
    cols = lax.broadcasted_iota(jnp.int32, (ROWS, ROWS), 1)

    def attend(st, block, masks, members=(0, 1)):
        for g in range(2):
            lanes = slice(g * HEAD_WIDTH, (g + 1) * HEAD_WIDTH)
            keys = block[:, 0, lanes]
            values = block[:, 1, lanes].T
            for mi in members:
                for u in range(2):
                    first = (2 * g + u) * HEAD_WIDTH
                    query = q_all[st, mi, :, first:first + HEAD_WIDTH]
                    c = (g * 2 + mi) * 2 + u
                    scores = lax.dot_general(
                        keys, query, (((1,), (1,)), ((), ())),
                        preferred_element_type=jnp.float32,
                    )
                    scores = jnp.where(masks[mi], scores, NEG)
                    old = m_ref[st, c:c + 1, :]
                    new = jnp.maximum(old, jnp.max(scores, axis=0, keepdims=True))
                    weights = jnp.exp2((scores - new) * SCALE2)
                    keep = jnp.exp2((old - new) * SCALE2)
                    m_ref[st, c:c + 1, :] = new
                    l_ref[st, c:c + 1, :] = l_ref[st, c:c + 1, :] * keep + jnp.sum(
                        weights, axis=0, keepdims=True
                    )
                    mixed = jnp.dot(
                        values, weights.astype(jnp.bfloat16),
                        preferred_element_type=jnp.float32,
                    )
                    acc[st, c] = acc[st, c] * keep + mixed

    member = x // 2
    mine = suffix_len[lax.rem(x, 2) * NZ + z]
    here = mine - member * ROWS
    local[1].wait()
    local[2].wait()
    q_copies[0].wait_recv()
    attend(
        0, skv,
        {0: (rows <= cols) & (rows < here), 1: rows < here * (1 - member)},
    )
    def unit(st, i, received):
        if received:
            remote(
                sending.at[i], kv.at[i], p_send.at[i], p_recv.at[i], partner
            ).wait_recv()
        mask = rows < table[PAGES + i]
        attend(st, kv.at[i], {0: mask, 1: mask})

    unit(0, SELF[0], False)
    q_copies[1].wait_recv()
    q_copies[2].wait_recv()
    unit(1, SELF[1], False)

    targets = ((0, 1, partner), (1, 0, node(*own_side_near)), (1, 1, node(*side_far)))
    o_copies = {}

    def give(n):
        st, mi, to = targets[n]
        for g in range(2):
            for u in range(2):
                c = (g * 2 + mi) * 2 + u
                share = l_ref[st, c:c + 1, :]
                o_out[g, n, u] = (acc[st, c] / share).astype(jnp.bfloat16)
                st_out[g, n, u:u + 1, :] = m_ref[st, c:c + 1, :]
                st_out[g, n, 2 + u:3 + u, :] = share
            e = g * 3 + n
            pair = (
                remote(st_out.at[g, n], st_in.at[g, n], t_send.at[e], t_recv.at[e], to),
                remote(o_out.at[g, n], o_in.at[g, n], o_send.at[e], o_recv.at[e], to),
            )
            for copy in pair:
                copy.start()
            o_copies[g, n] = pair

    def side_unit(i, carry):
        unit(1, i, True)
        return carry

    def home_unit(i, carry):
        unit(0, i, True)
        return carry

    lax.fori_loop(2, SIDE_END, side_unit, 0)
    give(2)
    give(1)
    lax.fori_loop(SIDE_END, PAGES, home_unit, 0)
    give(0)

    a_copies = {}
    live = lax.broadcasted_iota(jnp.int32, (1, ROWS), 1) < here
    for g in range(2):
        for n in range(3):
            for copy in o_copies[g, n]:
                copy.wait_recv()
        for u in range(2):
            c = g * 4 + u
            tops = [m_ref[0, c:c + 1, :]] + [st_in[g, n, u:u + 1, :] for n in range(3)]
            sums = [l_ref[0, c:c + 1, :]] + [st_in[g, n, 2 + u:3 + u, :] for n in range(3)]
            top = jnp.maximum(jnp.maximum(tops[0], tops[1]), jnp.maximum(tops[2], tops[3]))
            factors = [jnp.exp2((t - top) * SCALE2) for t in tops]
            shares = [f * l for f, l in zip(factors, sums)]
            whole = shares[0] + shares[1] + shares[2] + shares[3]
            inverse = jnp.where(live, 1.0 / whole, 0.0)
            value = acc[0, c] * (factors[0] * inverse)
            for n in range(3):
                value += o_in[g, n, u].astype(jnp.float32) * (shares[n + 1] * inverse)
            first = (2 * g + u) * HEAD_WIDTH
            attn[y, :, first:first + HEAD_WIDTH] = value.T.astype(jnp.bfloat16)
        half = pl.ds(g * 256, 256)
        for dy in (1, 3, 2):
            e = g * 3 + dy - 1
            copy = remote(
                attn.at[y, :, half], attn.at[y, :, half], a_send.at[e], a_recv.at[e], chip(dy)
            )
            copy.start()
            a_copies[g, dy] = copy

    own_weight.wait()
    total[...] = jnp.dot(attn[y], w_all[y], preferred_element_type=jnp.float32)
    for n, dy in enumerate((1, 3, 2)):
        w_copies[n].wait_recv()
    for g in range(2):
        for dy in (1, 3, 2):
            a_copies[g, dy].wait_recv()
            of = wrap(y - dy, NY)
            total[...] += jnp.dot(
                attn[of, :, g * 256:(g + 1) * 256], w_all[of, g * 256:(g + 1) * 256, :],
                preferred_element_type=jnp.float32,
            )

    def columns_of(c):
        return pltpu.roll(total[...], WIDE - 64 * lax.rem(y, 2) - DEV_COLS * c, 1)[:, :768]

    sib_out[...] = columns_of(1 - core).astype(jnp.bfloat16)
    swap = remote(sib_out, sib_in, b_send.at[0], b_recv.at[0], sibling)
    swap.start()
    own = columns_of(core)
    swap.wait_recv()
    out_ref[...] = (own + sib_in[...].astype(jnp.float32)).astype(jnp.bfloat16)[:, :DEV_COLS]

    for copy in q_copies + w_copies + p_copies + list(a_copies.values()) + [swap]:
        copy.wait_send()
    for pair in o_copies.values():
        for copy in pair:
            copy.wait_send()


def shards(queries, suffix_key_value, pooled_pages, out_weight, page_table, prefix_len, suffix_len):
    seq = lax.axis_index("seq")
    x, z = seq // NZ, lax.rem(seq, NZ)
    devices, requests = [], []
    for message in MESSAGES:
        devices.append(seq)
        requests.append(request_of(message, *dest_of(message, x, z)))
    for message in MESSAGES:
        xx, zz = source_of(message, x, z)
        devices.append(xx * NZ + zz)
        requests.append(request_of(message, x, z))
    devices = jnp.stack(devices)[:, None, None]
    requests = jnp.stack(requests)[:, None, None]
    request = jnp.arange(page_table.shape[0], dtype=jnp.int32)[None, :, None]
    position = jnp.arange(page_table.shape[1], dtype=jnp.int32)[None, None, :] * ROWS
    entry = jnp.arange(2 * PAGES, dtype=jnp.int32)[:, None, None]
    chosen = (request == requests) & (page_table[None] // PAGES == devices)
    value = jnp.where(
        entry < PAGES, page_table[None] % PAGES, prefix_len[None, :, None] - position
    )
    table = jnp.sum(jnp.where(chosen, value, 0), axis=(1, 2))

    vmem = pltpu.VMEM
    dma = pltpu.SemaphoreType.DMA
    bf16, f32 = jnp.bfloat16, jnp.float32
    return pl.pallas_call(
        kernel,
        out_shape=jax.ShapeDtypeStruct((ROWS, DEV_COLS), bf16),
        in_specs=[pl.BlockSpec(memory_space=pltpu.SMEM)] * 2
        + [pl.BlockSpec(memory_space=pl.ANY)] * 4,
        out_specs=pl.BlockSpec(memory_space=vmem),
        scratch_shapes=[
            vmem((PAGES, ROWS, 2, 256), bf16),
            vmem((PAGES, ROWS, 2, 256), bf16),
            vmem((PAGES, ROWS, 2, 256), bf16),
            vmem((ROWS, 2, 256), bf16),
            vmem((2, 2, ROWS, 512), bf16),
            vmem((NY, 512, WIDE), bf16),
            vmem((2, 8, HEAD_WIDTH, ROWS), f32),
            vmem((2, 8, ROWS), f32),
            vmem((2, 8, ROWS), f32),
            vmem((2, 3, 2, HEAD_WIDTH, ROWS), bf16),
            vmem((2, 3, 2, HEAD_WIDTH, ROWS), bf16),
            vmem((2, 3, 8, ROWS), f32),
            vmem((2, 3, 8, ROWS), f32),
            vmem((NY, ROWS, 512), bf16),
            vmem((ROWS, WIDE), f32),
            vmem((ROWS, 768), bf16),
            vmem((ROWS, 768), bf16),
            dma((4,)), dma((3,)), dma((3,)), dma((PAGES,)), dma((PAGES,)), dma((3,)), dma((3,)),
            dma((6,)), dma((6,)), dma((6,)), dma((6,)), dma((6,)), dma((6,)), dma((1,)), dma((1,)),
        ],
        compiler_params=pltpu.CompilerParams(
            collective_id=0, has_side_effects=True, vmem_limit_bytes=56 * 1024 * 1024
        ),
        name="paged_prefill",
    )(table, suffix_len, queries, suffix_key_value, pooled_pages, out_weight)


def solution(mesh):
    placed = (
        P("seq", "head"),
        P("seq", None, "head"),
        P("seq", None, None, "head"),
        P("head", None),
        P(),
        P(),
        P(),
    )
    return jax.shard_map(
        shards, mesh=mesh, in_specs=placed, out_specs=P("seq", "head"), check_vma=False
    )
```

```python
import functools

import jax
import jax.numpy as jnp
from jax import lax
from jax.experimental import pallas as pl
from jax.experimental.pallas import tpu as pltpu
from jax.sharding import PartitionSpec as P

D = 5376
QUERY_HEADS = 32
KEY_VALUE_HEADS = 16
HEAD_WIDTH = 128
NX, NZ, NY = 4, 8, 4
ROWS = 256
PAGES = 16
NEG = -1e30
SCALE2 = float(D // QUERY_HEADS) ** (-0.5) * 1.4426950408889634
CHIP_COLS = D // NY
WIDE = 1408
DEV_COLS = D // 8
MESH = pl.DeviceIdType.MESH

MESSAGES = (
    ("h", 0, 0), ("s", 0, 0),
    ("s", 1, 0), ("s", 3, 0), ("s", 0, 1), ("s", 2, 0), ("s", 0, 2),
    ("s", 1, 1), ("s", 3, 1), ("s", 3, 2), ("s", 2, 1),
    ("h", 0, 1), ("h", 0, -1), ("h", 1, 0), ("h", 1, 1), ("h", 1, -1),
)
SELF = (0, 1)
SIDE_END = 11


def sign(x, z):
    return 1 - 2 * lax.rem(x // 2 + z, 2)


def wrap(v, n):
    return lax.rem(v + 4 * n, n)


def home_step(j, dz):
    if j == 0:
        return 0, -dz
    return (-1, 0) if dz == 0 else (1, -dz)


def dest_of(message, x, z):
    kind, a, b = message
    if kind == "h":
        dx, dz = home_step(a, b)
        return wrap(x + dx, NX), wrap(z + dz, NZ)
    to = wrap(x + a, NX)
    return to, wrap(z - sign(to, z + b) * b, NZ)


def source_of(message, x, z):
    kind, a, b = message
    if kind == "h":
        dx, dz = home_step(a, b)
        return wrap(x - dx, NX), wrap(z - dz, NZ)
    return wrap(x - a, NX), wrap(z + sign(x, z) * b, NZ)


def request_of(message, x, z):
    if message[0] == "h":
        return lax.rem(x, 2) * NZ + z
    return lax.rem(x, 2) * NZ + wrap(z - 2 * sign(x, z), NZ)


def kernel(
    owners, prefix_len, suffix_len, q_hbm, skv_hbm, pages_hbm, w_hbm, out_ref,
    pages, sending, kv, skv, q_all, w_all, acc, m_ref, l_ref,
    o_out, o_in, st_out, st_in, attn, total, turned, sib_out, sib_in, slots, counts,
    local_sem, q_send, q_recv, p_send, p_recv, w_send, w_recv,
    o_send, o_recv, t_send, t_recv, a_send, a_recv, b_send, b_recv,
):
    seq = lax.axis_index("seq")
    head = lax.axis_index("head")
    x, z = seq // NZ, lax.rem(seq, NZ)
    y, core = head // 2, lax.rem(head, 2)
    s = sign(x, z)

    def node(xx, zz):
        return {"seq": xx * NZ + zz, "head": head}

    def chip(dy):
        return {"seq": seq, "head": wrap(y + dy, NY) * 2 + core}

    sibling = {"seq": seq, "head": y * 2 + 1 - core}
    partner = node(wrap(x + 2, NX), z)
    side_near = (x, wrap(z + 2 * s, NZ))
    side_far = (wrap(x + 2, NX), wrap(z - 2 * s, NZ))
    own_side_near = (x, wrap(z - 2 * s, NZ))

    local = [
        pltpu.make_async_copy(pages_hbm, pages, local_sem.at[0]),
        pltpu.make_async_copy(q_hbm, q_all.at[0, 0], local_sem.at[1]),
        pltpu.make_async_copy(skv_hbm, skv, local_sem.at[2]),
    ]
    for copy in local:
        copy.start()

    barrier = pltpu.get_barrier_semaphore()
    heard = 0
    for k, message in enumerate(MESSAGES):
        if k in SELF:
            continue
        pl.semaphore_signal(
            barrier, inc=1, device_id=node(*source_of(message, x, z)), device_id_type=MESH
        )
        heard += 1
    for where in (own_side_near, side_far):
        pl.semaphore_signal(barrier, inc=1, device_id=node(*where), device_id_type=MESH)
        heard += 1
    for dy in (1, 2, 3):
        pl.semaphore_signal(barrier, inc=1, device_id=chip(dy), device_id_type=MESH)
        heard += 1
    pl.semaphore_signal(barrier, inc=1, device_id=sibling, device_id_type=MESH)
    heard += 1

    acc[...] = jnp.zeros_like(acc)
    m_ref[...] = jnp.full(m_ref.shape, NEG, jnp.float32)
    l_ref[...] = jnp.zeros_like(l_ref)
    place = lax.broadcasted_iota(jnp.int32, (1, owners.shape[1]), 1) * ROWS
    for k, message in enumerate(MESSAGES):
        row = owners[pl.ds(request_of(message, *dest_of(message, x, z)), 1), :]
        slots[k] = jnp.sum(
            jnp.where(jnp.right_shift(row, 4) == seq, jnp.bitwise_and(row, PAGES - 1), 0)
        )
        served = request_of(message, x, z)
        xx, zz = source_of(message, x, z)
        row = owners[pl.ds(served, 1), :]
        counts[k] = jnp.sum(
            jnp.where(jnp.right_shift(row, 4) == xx * NZ + zz, prefix_len[served] - place, 0)
        )
    local[0].wait()

    def split(page, block):
        block[0] = page[:, 0, :]
        block[1] = page[:, 1, :].T

    def stage(first, last, buffer):
        def one(k, carry):
            split(pages[slots[k]], buffer.at[k])
            return carry

        lax.fori_loop(first, last, one, 0)

    stage(2, 6, sending)
    pl.semaphore_wait(barrier, heard)

    def remote(src, dst, send, recv, to):
        return pltpu.make_async_remote_copy(
            src_ref=src, dst_ref=dst, send_sem=send, recv_sem=recv,
            device_id=to, device_id_type=MESH,
        )

    q_copies = [
        remote(q_hbm, q_all.at[0, 1], q_send.at[0], q_recv.at[0], partner),
        remote(q_hbm, q_all.at[1, 0], q_send.at[1], q_recv.at[1], node(*side_near)),
        remote(q_hbm, q_all.at[1, 1], q_send.at[2], q_recv.at[2], node(*side_far)),
    ]
    for copy in q_copies:
        copy.start()

    def column(of):
        return pl.multiple_of(((21 * of) // 2) * 128, 128)

    own_weight = pltpu.make_async_copy(
        w_hbm.at[:, pl.ds(column(y), WIDE)], w_all.at[y], local_sem.at[3]
    )
    own_weight.start()
    w_copies = []
    for dy in (1, 3, 2):
        of = wrap(y + dy, NY)
        w_copies.append(
            remote(
                w_hbm.at[:, pl.ds(column(of), WIDE)], w_all.at[y],
                w_send.at[dy - 1], w_recv.at[dy - 1], chip(dy),
            )
        )
        w_copies[-1].start()

    p_copies = []
    for k, message in enumerate(MESSAGES):
        if k in SELF:
            continue
        if k == 6:
            stage(6, SIDE_END, sending)
        if k == SIDE_END:
            stage(SIDE_END, PAGES, sending)
        copy = remote(
            sending.at[k], kv.at[k], p_send.at[k], p_recv.at[k],
            node(*dest_of(message, x, z)),
        )
        copy.start()
        p_copies.append(copy)

    rows = lax.broadcasted_iota(jnp.int32, (ROWS, ROWS), 0)
    cols = lax.broadcasted_iota(jnp.int32, (ROWS, ROWS), 1)

    def attend(st, block, masks, members=(0, 1)):
        for g in range(2):
            lanes = slice(g * HEAD_WIDTH, (g + 1) * HEAD_WIDTH)
            keys = block[0, :, lanes]
            values = block[1, lanes, :]
            for mi in members:
                for u in range(2):
                    first = (2 * g + u) * HEAD_WIDTH
                    query = q_all[st, mi, :, first:first + HEAD_WIDTH]
                    c = (g * 2 + mi) * 2 + u
                    scores = lax.dot_general(
                        keys, query, (((1,), (1,)), ((), ())),
                        preferred_element_type=jnp.float32,
                    )
                    scores = jnp.where(masks[mi], scores, NEG)
                    old = m_ref[st, c:c + 1, :]
                    new = jnp.maximum(old, jnp.max(scores, axis=0, keepdims=True))
                    weights = jnp.exp2((scores - new) * SCALE2)
                    keep = jnp.exp2((old - new) * SCALE2)
                    m_ref[st, c:c + 1, :] = new
                    l_ref[st, c:c + 1, :] = l_ref[st, c:c + 1, :] * keep + jnp.sum(
                        weights, axis=0, keepdims=True
                    )
                    mixed = jnp.dot(
                        values, weights.astype(jnp.bfloat16),
                        preferred_element_type=jnp.float32,
                    )
                    acc[st, c] = acc[st, c] * keep + mixed

    member = x // 2
    mine = suffix_len[lax.rem(x, 2) * NZ + z]
    here = mine - member * ROWS
    stage(0, 2, kv)
    local[2].wait()
    split(skv[...], kv.at[PAGES])
    local[1].wait()
    own_mask = rows < counts[0]
    attend(0, kv.at[PAGES], {0: (rows <= cols) & (rows < here)}, (0,))
    attend(0, kv.at[0], {0: own_mask}, (0,))
    q_copies[0].wait_recv()
    attend(0, kv.at[PAGES], {1: rows < here * (1 - member)}, (1,))
    attend(0, kv.at[0], {1: own_mask}, (1,))
    def unit(st, i):
        @pl.when(i != SELF[1])
        def _():
            remote(
                sending.at[i], kv.at[i], p_send.at[i], p_recv.at[i], partner
            ).wait_recv()

        mask = rows < counts[i]
        attend(st, kv.at[i], {0: mask, 1: mask})

    q_copies[1].wait_recv()
    q_copies[2].wait_recv()

    targets = ((0, 1, partner), (1, 0, node(*own_side_near)), (1, 1, node(*side_far)))
    o_copies = {}

    def give(n):
        st, mi, to = targets[n]
        for g in range(2):
            for u in range(2):
                c = (g * 2 + mi) * 2 + u
                share = l_ref[st, c:c + 1, :]
                o_out[g, n, u] = (acc[st, c] * (1.0 / share)).astype(jnp.bfloat16)
                st_out[g, n, u:u + 1, :] = m_ref[st, c:c + 1, :]
                st_out[g, n, 2 + u:3 + u, :] = share
            e = g * 3 + n
            pair = (
                remote(st_out.at[g, n], st_in.at[g, n], t_send.at[e], t_recv.at[e], to),
                remote(o_out.at[g, n], o_in.at[g, n], o_send.at[e], o_recv.at[e], to),
            )
            for copy in pair:
                copy.start()
            o_copies[g, n] = pair

    def side_unit(i, carry):
        unit(1, i)
        return carry

    def home_unit(i, carry):
        unit(0, i)
        return carry

    lax.fori_loop(SELF[1], SIDE_END, side_unit, 0)
    give(2)
    give(1)
    lax.fori_loop(SIDE_END, PAGES, home_unit, 0)
    give(0)

    a_copies = {}
    live = lax.broadcasted_iota(jnp.int32, (1, ROWS), 1) < here
    for g in range(2):
        for n in range(3):
            for copy in o_copies[g, n]:
                copy.wait_recv()
        for u in range(2):
            c = g * 4 + u
            tops = [m_ref[0, c:c + 1, :]] + [st_in[g, n, u:u + 1, :] for n in range(3)]
            sums = [l_ref[0, c:c + 1, :]] + [st_in[g, n, 2 + u:3 + u, :] for n in range(3)]
            top = jnp.maximum(jnp.maximum(tops[0], tops[1]), jnp.maximum(tops[2], tops[3]))
            factors = [jnp.exp2((t - top) * SCALE2) for t in tops]
            shares = [f * l for f, l in zip(factors, sums)]
            whole = shares[0] + shares[1] + shares[2] + shares[3]
            inverse = jnp.where(live, 1.0 / whole, 0.0)
            value = acc[0, c] * (factors[0] * inverse)
            for n in range(3):
                value += o_in[g, n, u].astype(jnp.float32) * (shares[n + 1] * inverse)
            first = (2 * g + u) * HEAD_WIDTH
            attn[y, :, first:first + HEAD_WIDTH] = value.T.astype(jnp.bfloat16)
        half = pl.ds(g * 256, 256)
        for dy in (1, 3, 2):
            e = g * 3 + dy - 1
            copy = remote(
                attn.at[y, :, half], attn.at[y, :, half], a_send.at[e], a_recv.at[e], chip(dy)
            )
            copy.start()
            a_copies[g, dy] = copy

    own_weight.wait()
    total[...] = jnp.dot(attn[y], w_all[y], preferred_element_type=jnp.float32)
    for n, dy in enumerate((1, 3, 2)):
        w_copies[n].wait_recv()
    for g in range(2):
        for dy in (1, 3, 2):
            a_copies[g, dy].wait_recv()
            of = wrap(y - dy, NY)
            total[...] += jnp.dot(
                attn[of, :, g * 256:(g + 1) * 256], w_all[of, g * 256:(g + 1) * 256, :],
                preferred_element_type=jnp.float32,
            )

    turned[...] = total[...].T

    def columns_of(c):
        first = 64 * lax.rem(y, 2) + DEV_COLS * c
        return turned[pl.ds(pl.multiple_of(first, 32), DEV_COLS), :]

    sib_out[...] = columns_of(1 - core).astype(jnp.bfloat16)
    swap = remote(sib_out, sib_in, b_send.at[0], b_recv.at[0], sibling)
    swap.start()
    own = columns_of(core)
    swap.wait_recv()
    out_ref[...] = (own + sib_in[...].astype(jnp.float32)).astype(jnp.bfloat16)

    for copy in q_copies + w_copies + p_copies + list(a_copies.values()) + [swap]:
        copy.wait_send()
    for pair in o_copies.values():
        for copy in pair:
            copy.wait_send()


def shards(queries, suffix_key_value, pooled_pages, out_weight, page_table, prefix_len, suffix_len):
    vmem = pltpu.VMEM
    dma = pltpu.SemaphoreType.DMA
    bf16, f32 = jnp.bfloat16, jnp.float32
    return pl.pallas_call(
        kernel,
        out_shape=jax.ShapeDtypeStruct((DEV_COLS, ROWS), bf16),
        in_specs=[pl.BlockSpec(memory_space=vmem)]
        + [pl.BlockSpec(memory_space=pltpu.SMEM)] * 2
        + [pl.BlockSpec(memory_space=pl.ANY)] * 4,
        out_specs=pl.BlockSpec(memory_space=vmem),
        scratch_shapes=[
            vmem((PAGES, ROWS, 2, 256), bf16),
            vmem((PAGES, 2, ROWS, 256), bf16),
            vmem((PAGES + 1, 2, ROWS, 256), bf16),
            vmem((ROWS, 2, 256), bf16),
            vmem((2, 2, ROWS, 512), bf16),
            vmem((NY, 512, WIDE), bf16),
            vmem((2, 8, HEAD_WIDTH, ROWS), f32),
            vmem((2, 8, ROWS), f32),
            vmem((2, 8, ROWS), f32),
            vmem((2, 3, 2, HEAD_WIDTH, ROWS), bf16),
            vmem((2, 3, 2, HEAD_WIDTH, ROWS), bf16),
            vmem((2, 3, 8, ROWS), f32),
            vmem((2, 3, 8, ROWS), f32),
            vmem((NY, ROWS, 512), bf16),
            vmem((ROWS, WIDE), f32),
            vmem((WIDE, ROWS), f32),
            vmem((DEV_COLS, ROWS), bf16),
            vmem((DEV_COLS, ROWS), bf16),
            pltpu.SMEM((PAGES,), jnp.int32),
            pltpu.SMEM((PAGES,), jnp.int32),
            dma((4,)), dma((3,)), dma((3,)), dma((PAGES,)), dma((PAGES,)), dma((3,)), dma((3,)),
            dma((6,)), dma((6,)), dma((6,)), dma((6,)), dma((6,)), dma((6,)), dma((1,)), dma((1,)),
        ],
        compiler_params=pltpu.CompilerParams(
            collective_id=0, has_side_effects=True, vmem_limit_bytes=56 * 1024 * 1024
        ),
        name="paged_prefill",
    )(
        page_table, prefix_len, suffix_len, queries, suffix_key_value, pooled_pages, out_weight
    ).T


def solution(mesh):
    placed = (
        P("seq", "head"),
        P("seq", None, "head"),
        P("seq", None, None, "head"),
        P("head", None),
        P(),
        P(),
        P(),
    )
    return jax.shard_map(
        shards, mesh=mesh, in_specs=placed, out_specs=P("seq", "head"), check_vma=False
    )
```

```python
import functools

import jax
import jax.numpy as jnp
from jax import lax
from jax.experimental import pallas as pl
from jax.experimental.pallas import tpu as pltpu
from jax.sharding import PartitionSpec as P

D = 5376
QUERY_HEADS = 32
KEY_VALUE_HEADS = 16
HEAD_WIDTH = 128
NX, NZ, NY = 4, 8, 4
ROWS = 256
PAGES = 16
NEG = -1e30
SCALE2 = float(D // QUERY_HEADS) ** (-0.5) * 1.4426950408889634
CHIP_COLS = D // NY
WIDE = 1408
DEV_COLS = D // 8
MESH = pl.DeviceIdType.MESH

MESSAGES = (
    ("h", 0, 0), ("s", 0, 0),
    ("s", 0, 2), ("s", 2, 0), ("s", 2, 1), ("s", 3, 2), ("s", 1, 1),
    ("s", 3, 1), ("s", 0, 1), ("s", 1, 0), ("s", 3, 0),
    ("h", 1, 1), ("h", 1, -1), ("h", 1, 0), ("h", 0, 1), ("h", 0, -1),
)
SELF = (0, 1)
SIDE_END = 11
FLIGHT = 8
EARLY = 3


def sign(x, z):
    return 1 - 2 * lax.rem(x // 2 + z, 2)


def wrap(v, n):
    return lax.rem(v + 4 * n, n)


def home_step(j, dz):
    if j == 0:
        return 0, -dz
    return (-1, 0) if dz == 0 else (1, -dz)


def dest_of(message, x, z):
    kind, a, b = message
    if kind == "h":
        dx, dz = home_step(a, b)
        return wrap(x + dx, NX), wrap(z + dz, NZ)
    to = wrap(x + a, NX)
    return to, wrap(z - sign(to, z + b) * b, NZ)


def source_of(message, x, z):
    kind, a, b = message
    if kind == "h":
        dx, dz = home_step(a, b)
        return wrap(x - dx, NX), wrap(z - dz, NZ)
    return wrap(x - a, NX), wrap(z + sign(x, z) * b, NZ)


def request_of(message, x, z):
    if message[0] == "h":
        return lax.rem(x, 2) * NZ + z
    return lax.rem(x, 2) * NZ + wrap(z - 2 * sign(x, z), NZ)


def kernel(
    owners, prefix_len, suffix_len, q_hbm, skv_hbm, pages_hbm, w_hbm, out_ref,
    pages, sending, kv, skv, q_all, w_all, acc, m_ref, l_ref,
    o_out, o_in, st_out, st_in, attn, total, turned, sib_out, sib_in, slots, counts,
    local_sem, q_send, q_recv, p_send, p_recv, w_send, w_recv,
    o_send, o_recv, t_send, t_recv, a_send, a_recv, b_send, b_recv,
):
    seq = lax.axis_index("seq")
    head = lax.axis_index("head")
    x, z = seq // NZ, lax.rem(seq, NZ)
    y, core = head // 2, lax.rem(head, 2)
    s = sign(x, z)

    def node(xx, zz):
        return {"seq": xx * NZ + zz, "head": head}

    def chip(dy):
        return {"seq": seq, "head": wrap(y + dy, NY) * 2 + core}

    sibling = {"seq": seq, "head": y * 2 + 1 - core}
    partner = node(wrap(x + 2, NX), z)
    side_near = (x, wrap(z + 2 * s, NZ))
    side_far = (wrap(x + 2, NX), wrap(z - 2 * s, NZ))
    own_side_near = (x, wrap(z - 2 * s, NZ))

    local = [
        pltpu.make_async_copy(pages_hbm, pages, local_sem.at[0]),
        pltpu.make_async_copy(q_hbm, q_all.at[0, 0], local_sem.at[1]),
        pltpu.make_async_copy(skv_hbm, skv, local_sem.at[2]),
    ]
    for copy in local:
        copy.start()

    barrier = pltpu.get_barrier_semaphore()
    heard = 0
    for k, message in enumerate(MESSAGES):
        if k in SELF:
            continue
        pl.semaphore_signal(
            barrier, inc=1, device_id=node(*source_of(message, x, z)), device_id_type=MESH
        )
        heard += 1
    for where in (own_side_near, side_far):
        pl.semaphore_signal(barrier, inc=1, device_id=node(*where), device_id_type=MESH)
        heard += 1
    for dy in (1, 2, 3):
        pl.semaphore_signal(barrier, inc=1, device_id=chip(dy), device_id_type=MESH)
        heard += 1
    pl.semaphore_signal(barrier, inc=1, device_id=sibling, device_id_type=MESH)
    heard += 1

    acc[...] = jnp.zeros_like(acc)
    m_ref[...] = jnp.full(m_ref.shape, NEG, jnp.float32)
    l_ref[...] = jnp.zeros_like(l_ref)
    place = lax.broadcasted_iota(jnp.int32, (1, owners.shape[1]), 1) * ROWS
    for k, message in enumerate(MESSAGES):
        row = owners[pl.ds(request_of(message, *dest_of(message, x, z)), 1), :]
        slots[k] = jnp.sum(
            jnp.where(jnp.right_shift(row, 4) == seq, jnp.bitwise_and(row, PAGES - 1), 0)
        )
        served = request_of(message, x, z)
        xx, zz = source_of(message, x, z)
        row = owners[pl.ds(served, 1), :]
        counts[k] = jnp.sum(
            jnp.where(jnp.right_shift(row, 4) == xx * NZ + zz, prefix_len[served] - place, 0)
        )
    local[0].wait()

    def split(page, block):
        block[0] = page[:, 0, :]
        block[1] = page[:, 1, :].T

    def stage(first, last, buffer):
        def one(k, carry):
            split(pages[slots[k]], buffer.at[k])
            return carry

        lax.fori_loop(first, last, one, 0)

    stage(2, 6, sending)
    pl.semaphore_wait(barrier, heard)

    def remote(src, dst, send, recv, to):
        return pltpu.make_async_remote_copy(
            src_ref=src, dst_ref=dst, send_sem=send, recv_sem=recv,
            device_id=to, device_id_type=MESH,
        )

    q_copies = [
        remote(q_hbm, q_all.at[0, 1], q_send.at[0], q_recv.at[0], partner),
        remote(q_hbm, q_all.at[1, 0], q_send.at[1], q_recv.at[1], node(*side_near)),
        remote(q_hbm, q_all.at[1, 1], q_send.at[2], q_recv.at[2], node(*side_far)),
    ]
    for copy in q_copies:
        copy.start()

    def column(of):
        return pl.multiple_of(((21 * of) // 2) * 128, 128)

    own_weight = pltpu.make_async_copy(
        w_hbm.at[:, pl.ds(column(y), WIDE)], w_all.at[y], local_sem.at[3]
    )
    own_weight.start()
    w_copies = []
    for dy in (1, 3, 2):
        of = wrap(y + dy, NY)
        w_copies.append(
            remote(
                w_hbm.at[:, pl.ds(column(of), WIDE)], w_all.at[y],
                w_send.at[dy - 1], w_recv.at[dy - 1], chip(dy),
            )
        )
        w_copies[-1].start()

    p_copies = []
    for k, message in enumerate(MESSAGES):
        p_copies.append(
            remote(
                sending.at[k], kv.at[k], p_send.at[k], p_recv.at[k],
                node(*dest_of(message, x, z)),
            )
        )
    for k in range(2, 2 + EARLY):
        p_copies[k].start()
    stage(6, SIDE_END, sending)
    stage(SIDE_END, PAGES, sending)
    for k in range(2 + EARLY, 2 + FLIGHT):
        p_copies[k].start()

    rows = lax.broadcasted_iota(jnp.int32, (ROWS, ROWS), 0)
    cols = lax.broadcasted_iota(jnp.int32, (ROWS, ROWS), 1)

    def attend(st, block, masks, members=(0, 1)):
        for g in range(2):
            lanes = slice(g * HEAD_WIDTH, (g + 1) * HEAD_WIDTH)
            keys = block[0, :, lanes]
            values = block[1, lanes, :]
            parts = [(mi, u) for mi in members for u in range(2)]
            scores, olds = [], []
            for mi, u in parts:
                first = (2 * g + u) * HEAD_WIDTH
                raw = lax.dot_general(
                    keys, q_all[st, mi, :, first:first + HEAD_WIDTH],
                    (((1,), (1,)), ((), ())), preferred_element_type=jnp.float32,
                )
                scores.append(jnp.where(masks[mi], raw, NEG))
                c = (g * 2 + mi) * 2 + u
                olds.append((m_ref[st, c:c + 1, :], l_ref[st, c:c + 1, :]))
            results = []
            for score, (old, share) in zip(scores, olds):
                new = jnp.maximum(old, jnp.max(score, axis=0, keepdims=True))
                weights = jnp.exp2((score - new) * SCALE2)
                keep = jnp.exp2((old - new) * SCALE2)
                share = share * keep + jnp.sum(weights, axis=0, keepdims=True)
                mixed = jnp.dot(
                    values, weights.astype(jnp.bfloat16), preferred_element_type=jnp.float32
                )
                results.append((new, share, keep, mixed))
            for (mi, u), (new, share, keep, mixed) in zip(parts, results):
                c = (g * 2 + mi) * 2 + u
                m_ref[st, c:c + 1, :] = new
                l_ref[st, c:c + 1, :] = share
                acc[st, c] = acc[st, c] * keep + mixed

    member = x // 2
    mine = suffix_len[lax.rem(x, 2) * NZ + z]
    here = mine - member * ROWS
    stage(0, 2, kv)
    local[2].wait()
    split(skv[...], kv.at[PAGES])
    local[1].wait()
    own_mask = rows < counts[0]
    attend(0, kv.at[PAGES], {0: (rows <= cols) & (rows < here)}, (0,))
    attend(0, kv.at[0], {0: own_mask}, (0,))
    q_copies[0].wait_recv()
    attend(0, kv.at[PAGES], {1: rows < here * (1 - member)}, (1,))
    attend(0, kv.at[0], {1: own_mask}, (1,))
    def unit(st, i):
        @pl.when(i != SELF[1])
        def _():
            remote(
                sending.at[i], kv.at[i], p_send.at[i], p_recv.at[i], partner
            ).wait_recv()

        for k in range(2 + FLIGHT, PAGES):
            @pl.when(i == k - FLIGHT)
            def _():
                p_copies[k].start()

        mask = rows < counts[i]
        attend(st, kv.at[i], {0: mask, 1: mask})

    q_copies[1].wait_recv()
    q_copies[2].wait_recv()

    targets = ((0, 1, partner), (1, 0, node(*own_side_near)), (1, 1, node(*side_far)))
    o_copies = {}

    def give(n):
        st, mi, to = targets[n]
        for g in range(2):
            for u in range(2):
                c = (g * 2 + mi) * 2 + u
                share = l_ref[st, c:c + 1, :]
                o_out[g, n, u] = (acc[st, c] * (1.0 / share)).astype(jnp.bfloat16)
                st_out[g, n, u:u + 1, :] = m_ref[st, c:c + 1, :]
                st_out[g, n, 2 + u:3 + u, :] = share
            e = g * 3 + n
            pair = (
                remote(st_out.at[g, n], st_in.at[g, n], t_send.at[e], t_recv.at[e], to),
                remote(o_out.at[g, n], o_in.at[g, n], o_send.at[e], o_recv.at[e], to),
            )
            for copy in pair:
                copy.start()
            o_copies[g, n] = pair

    def side_unit(i, carry):
        unit(1, i)
        return carry

    def home_unit(i, carry):
        unit(0, i)
        return carry

    lax.fori_loop(SELF[1], SIDE_END, side_unit, 0)
    give(2)
    give(1)
    lax.fori_loop(SIDE_END, PAGES, home_unit, 0)
    give(0)

    a_copies = {}
    live = lax.broadcasted_iota(jnp.int32, (1, ROWS), 1) < here
    for g in range(2):
        for n in range(3):
            for copy in o_copies[g, n]:
                copy.wait_recv()
        for u in range(2):
            c = g * 4 + u
            tops = [m_ref[0, c:c + 1, :]] + [st_in[g, n, u:u + 1, :] for n in range(3)]
            sums = [l_ref[0, c:c + 1, :]] + [st_in[g, n, 2 + u:3 + u, :] for n in range(3)]
            top = jnp.maximum(jnp.maximum(tops[0], tops[1]), jnp.maximum(tops[2], tops[3]))
            factors = [jnp.exp2((t - top) * SCALE2) for t in tops]
            shares = [f * l for f, l in zip(factors, sums)]
            whole = shares[0] + shares[1] + shares[2] + shares[3]
            inverse = jnp.where(live, 1.0 / whole, 0.0)
            value = acc[0, c] * (factors[0] * inverse)
            for n in range(3):
                value += o_in[g, n, u].astype(jnp.float32) * (shares[n + 1] * inverse)
            first = (2 * g + u) * HEAD_WIDTH
            attn[y, :, first:first + HEAD_WIDTH] = value.T.astype(jnp.bfloat16)
        half = pl.ds(g * 256, 256)
        for dy in (1, 3, 2):
            e = g * 3 + dy - 1
            copy = remote(
                attn.at[y, :, half], attn.at[y, :, half], a_send.at[e], a_recv.at[e], chip(dy)
            )
            copy.start()
            a_copies[g, dy] = copy

    own_weight.wait()
    total[...] = jnp.dot(attn[y], w_all[y], preferred_element_type=jnp.float32)
    for n, dy in enumerate((1, 3, 2)):
        w_copies[n].wait_recv()
    for g in range(2):
        for dy in (1, 3, 2):
            a_copies[g, dy].wait_recv()
            of = wrap(y - dy, NY)
            total[...] += jnp.dot(
                attn[of, :, g * 256:(g + 1) * 256], w_all[of, g * 256:(g + 1) * 256, :],
                preferred_element_type=jnp.float32,
            )

    turned[...] = total[...].T

    def columns_of(c):
        first = 64 * lax.rem(y, 2) + DEV_COLS * c
        return turned[pl.ds(pl.multiple_of(first, 32), DEV_COLS), :]

    sib_out[...] = columns_of(1 - core).astype(jnp.bfloat16)
    swap = remote(sib_out, sib_in, b_send.at[0], b_recv.at[0], sibling)
    swap.start()
    own = columns_of(core)
    swap.wait_recv()
    out_ref[...] = (own + sib_in[...].astype(jnp.float32)).astype(jnp.bfloat16)

    for copy in q_copies + w_copies + p_copies[2:] + list(a_copies.values()) + [swap]:
        copy.wait_send()
    for pair in o_copies.values():
        for copy in pair:
            copy.wait_send()


def shards(queries, suffix_key_value, pooled_pages, out_weight, page_table, prefix_len, suffix_len):
    vmem = pltpu.VMEM
    dma = pltpu.SemaphoreType.DMA
    bf16, f32 = jnp.bfloat16, jnp.float32
    return pl.pallas_call(
        kernel,
        out_shape=jax.ShapeDtypeStruct((DEV_COLS, ROWS), bf16),
        in_specs=[pl.BlockSpec(memory_space=vmem)]
        + [pl.BlockSpec(memory_space=pltpu.SMEM)] * 2
        + [pl.BlockSpec(memory_space=pl.ANY)] * 4,
        out_specs=pl.BlockSpec(memory_space=vmem),
        scratch_shapes=[
            vmem((PAGES, ROWS, 2, 256), bf16),
            vmem((PAGES, 2, ROWS, 256), bf16),
            vmem((PAGES + 1, 2, ROWS, 256), bf16),
            vmem((ROWS, 2, 256), bf16),
            vmem((2, 2, ROWS, 512), bf16),
            vmem((NY, 512, WIDE), bf16),
            vmem((2, 8, HEAD_WIDTH, ROWS), f32),
            vmem((2, 8, ROWS), f32),
            vmem((2, 8, ROWS), f32),
            vmem((2, 3, 2, HEAD_WIDTH, ROWS), bf16),
            vmem((2, 3, 2, HEAD_WIDTH, ROWS), bf16),
            vmem((2, 3, 8, ROWS), f32),
            vmem((2, 3, 8, ROWS), f32),
            vmem((NY, ROWS, 512), bf16),
            vmem((ROWS, WIDE), f32),
            vmem((WIDE, ROWS), f32),
            vmem((DEV_COLS, ROWS), bf16),
            vmem((DEV_COLS, ROWS), bf16),
            pltpu.SMEM((PAGES,), jnp.int32),
            pltpu.SMEM((PAGES,), jnp.int32),
            dma((4,)), dma((3,)), dma((3,)), dma((PAGES,)), dma((PAGES,)), dma((3,)), dma((3,)),
            dma((6,)), dma((6,)), dma((6,)), dma((6,)), dma((6,)), dma((6,)), dma((1,)), dma((1,)),
        ],
        compiler_params=pltpu.CompilerParams(
            collective_id=0, has_side_effects=True, vmem_limit_bytes=56 * 1024 * 1024
        ),
        name="paged_prefill",
    )(
        page_table, prefix_len, suffix_len, queries, suffix_key_value, pooled_pages, out_weight
    ).T


def solution(mesh):
    placed = (
        P("seq", "head"),
        P("seq", None, "head"),
        P("seq", None, None, "head"),
        P("head", None),
        P(),
        P(),
        P(),
    )
    return jax.shard_map(
        shards, mesh=mesh, in_specs=placed, out_specs=P("seq", "head"), check_vma=False
    )
```

```python
import functools

import jax
import jax.numpy as jnp
from jax import lax
from jax.experimental import pallas as pl
from jax.experimental.pallas import tpu as pltpu
from jax.sharding import PartitionSpec as P

D = 5376
QUERY_HEADS = 32
KEY_VALUE_HEADS = 16
HEAD_WIDTH = 128
NX, NZ, NY = 4, 8, 4
ROWS = 256
PAGES = 16
NEG = -1e30
SCALE2 = float(D // QUERY_HEADS) ** (-0.5) * 1.4426950408889634
CHIP_COLS = D // NY
WIDE = 1408
DEV_COLS = D // 8
MESH = pl.DeviceIdType.MESH

MESSAGES = (
    ("h", 0, 0),
    ("s", 0, 0),
    ("s", 0, 2),
    ("s", 1, 0),
    ("s", 3, 0),
    ("s", 0, 1),
    ("s", 2, 0),
    ("s", 1, 1),
    ("s", 3, 1),
    ("s", 3, 2),
    ("s", 2, 1),
    ("h", 0, 1),
    ("h", 0, -1),
    ("h", 1, 0),
    ("h", 1, 1),
    ("h", 1, -1),
)
SELF = (0, 1)
SIDE_END = 11
FLIGHT = 10
EARLY = 3


def sign(x, z):
    return 1 - 2 * lax.rem(x // 2 + z, 2)


def wrap(v, n):
    return lax.rem(v + 4 * n, n)


def home_step(j, dz):
    if j == 0:
        return 0, -dz
    return (-1, 0) if dz == 0 else (1, -dz)


def dest_of(message, x, z):
    kind, a, b = message
    if kind == "h":
        dx, dz = home_step(a, b)
        return wrap(x + dx, NX), wrap(z + dz, NZ)
    to = wrap(x + a, NX)
    return to, wrap(z - sign(to, z + b) * b, NZ)


def source_of(message, x, z):
    kind, a, b = message
    if kind == "h":
        dx, dz = home_step(a, b)
        return wrap(x - dx, NX), wrap(z - dz, NZ)
    return wrap(x - a, NX), wrap(z + sign(x, z) * b, NZ)


def request_of(message, x, z):
    if message[0] == "h":
        return lax.rem(x, 2) * NZ + z
    return lax.rem(x, 2) * NZ + wrap(z - 2 * sign(x, z), NZ)


def kernel(
    owners, prefix_len, suffix_len, q_hbm, skv_hbm, pages_hbm, w_hbm, out_ref,
    pages, sending, kv, skv, q_all, w_all, acc, m_ref, l_ref,
    o_out, o_in, st_out, st_in, attn, total, turned, sib_out, sib_in, slots, counts,
    local_sem, q_send, q_recv, p_send, p_recv, w_send, w_recv,
    o_send, o_recv, t_send, t_recv, a_send, a_recv, b_send, b_recv,
):
    seq = lax.axis_index("seq")
    head = lax.axis_index("head")
    x, z = seq // NZ, lax.rem(seq, NZ)
    y, core = head // 2, lax.rem(head, 2)
    s = sign(x, z)

    def node(xx, zz):
        return {"seq": xx * NZ + zz, "head": head}

    def chip(dy):
        return {"seq": seq, "head": wrap(y + dy, NY) * 2 + core}

    sibling = {"seq": seq, "head": y * 2 + 1 - core}
    partner = node(wrap(x + 2, NX), z)
    side_near = (x, wrap(z + 2 * s, NZ))
    side_far = (wrap(x + 2, NX), wrap(z - 2 * s, NZ))
    own_side_near = (x, wrap(z - 2 * s, NZ))

    local = [
        pltpu.make_async_copy(pages_hbm, pages, local_sem.at[0]),
        pltpu.make_async_copy(q_hbm, q_all.at[0, 0], local_sem.at[1]),
        pltpu.make_async_copy(skv_hbm, skv, local_sem.at[2]),
    ]
    for copy in local:
        copy.start()

    barrier = pltpu.get_barrier_semaphore()
    heard = 0
    for k, message in enumerate(MESSAGES):
        if k in SELF:
            continue
        pl.semaphore_signal(
            barrier, inc=1, device_id=node(*source_of(message, x, z)), device_id_type=MESH
        )
        heard += 1
    for where in (own_side_near, side_far):
        pl.semaphore_signal(barrier, inc=1, device_id=node(*where), device_id_type=MESH)
        heard += 1
    for dy in (1, 2, 3):
        pl.semaphore_signal(barrier, inc=1, device_id=chip(dy), device_id_type=MESH)
        heard += 1
    pl.semaphore_signal(barrier, inc=1, device_id=sibling, device_id_type=MESH)
    heard += 1

    acc[...] = jnp.zeros_like(acc)
    m_ref[...] = jnp.full(m_ref.shape, NEG, jnp.float32)
    l_ref[...] = jnp.zeros_like(l_ref)
    place = lax.broadcasted_iota(jnp.int32, (1, owners.shape[1]), 1) * ROWS
    for k, message in enumerate(MESSAGES):
        row = owners[pl.ds(request_of(message, *dest_of(message, x, z)), 1), :]
        slots[k] = jnp.sum(
            jnp.where(jnp.right_shift(row, 4) == seq, jnp.bitwise_and(row, PAGES - 1), 0)
        )
        served = request_of(message, x, z)
        xx, zz = source_of(message, x, z)
        row = owners[pl.ds(served, 1), :]
        counts[k] = jnp.sum(
            jnp.where(jnp.right_shift(row, 4) == xx * NZ + zz, prefix_len[served] - place, 0)
        )
    local[0].wait()

    def split(page, block):
        block[0] = page[:, 0, :]
        block[1] = page[:, 1, :].T

    def stage(first, last, buffer):
        def one(k, carry):
            split(pages[slots[k]], buffer.at[k])
            return carry

        lax.fori_loop(first, last, one, 0)

    stage(2, 6, sending)
    pl.semaphore_wait(barrier, heard)

    def remote(src, dst, send, recv, to):
        return pltpu.make_async_remote_copy(
            src_ref=src, dst_ref=dst, send_sem=send, recv_sem=recv,
            device_id=to, device_id_type=MESH,
        )

    q_copies = [
        remote(q_hbm, q_all.at[0, 1], q_send.at[0], q_recv.at[0], partner),
        remote(q_hbm, q_all.at[1, 0], q_send.at[1], q_recv.at[1], node(*side_near)),
        remote(q_hbm, q_all.at[1, 1], q_send.at[2], q_recv.at[2], node(*side_far)),
    ]
    for copy in q_copies:
        copy.start()

    def column(of):
        return pl.multiple_of(((21 * of) // 2) * 128, 128)

    own_weight = pltpu.make_async_copy(
        w_hbm.at[:, pl.ds(column(y), WIDE)], w_all.at[y], local_sem.at[3]
    )
    own_weight.start()
    w_copies = []
    for dy in (1, 3, 2):
        of = wrap(y + dy, NY)
        w_copies.append(
            remote(
                w_hbm.at[:, pl.ds(column(of), WIDE)], w_all.at[y],
                w_send.at[dy - 1], w_recv.at[dy - 1], chip(dy),
            )
        )
        w_copies[-1].start()

    p_copies = []
    for k, message in enumerate(MESSAGES):
        p_copies.append(
            remote(
                sending.at[k], kv.at[k], p_send.at[k], p_recv.at[k],
                node(*dest_of(message, x, z)),
            )
        )
    for k in range(2, 2 + EARLY):
        p_copies[k].start()
    stage(6, SIDE_END, sending)
    stage(SIDE_END, PAGES, sending)
    for k in range(2 + EARLY, 2 + FLIGHT):
        p_copies[k].start()

    rows = lax.broadcasted_iota(jnp.int32, (ROWS, ROWS), 0)
    cols = lax.broadcasted_iota(jnp.int32, (ROWS, ROWS), 1)

    def attend(st, block, masks, members=(0, 1)):
        for g in range(2):
            lanes = slice(g * HEAD_WIDTH, (g + 1) * HEAD_WIDTH)
            keys = block[0, :, lanes]
            values = block[1, lanes, :]
            parts = [(mi, u) for mi in members for u in range(2)]
            scores, olds = [], []
            for mi, u in parts:
                first = (2 * g + u) * HEAD_WIDTH
                raw = lax.dot_general(
                    keys, q_all[st, mi, :, first:first + HEAD_WIDTH],
                    (((1,), (1,)), ((), ())), preferred_element_type=jnp.float32,
                )
                scores.append(jnp.where(masks[mi], raw, NEG))
                c = (g * 2 + mi) * 2 + u
                olds.append((m_ref[st, c:c + 1, :], l_ref[st, c:c + 1, :]))
            results = []
            for score, (old, share) in zip(scores, olds):
                new = jnp.maximum(old, jnp.max(score, axis=0, keepdims=True))
                weights = jnp.exp2((score - new) * SCALE2)
                keep = jnp.exp2((old - new) * SCALE2)
                share = share * keep + jnp.sum(weights, axis=0, keepdims=True)
                mixed = jnp.dot(
                    values, weights.astype(jnp.bfloat16), preferred_element_type=jnp.float32
                )
                results.append((new, share, keep, mixed))
            for (mi, u), (new, share, keep, mixed) in zip(parts, results):
                c = (g * 2 + mi) * 2 + u
                m_ref[st, c:c + 1, :] = new
                l_ref[st, c:c + 1, :] = share
                acc[st, c] = acc[st, c] * keep + mixed

    member = x // 2
    mine = suffix_len[lax.rem(x, 2) * NZ + z]
    here = mine - member * ROWS
    stage(0, 2, kv)
    local[2].wait()
    split(skv[...], kv.at[PAGES])
    local[1].wait()
    own_mask = rows < counts[0]
    attend(0, kv.at[PAGES], {0: (rows <= cols) & (rows < here)}, (0,))
    attend(0, kv.at[0], {0: own_mask}, (0,))
    q_copies[0].wait_recv()
    attend(0, kv.at[PAGES], {1: rows < here * (1 - member)}, (1,))
    attend(0, kv.at[0], {1: own_mask}, (1,))
    def unit(st, i):
        @pl.when(i != SELF[1])
        def _():
            remote(
                sending.at[i], kv.at[i], p_send.at[i], p_recv.at[i], partner
            ).wait_recv()

        for k in range(2 + FLIGHT, PAGES):
            @pl.when(i == k - FLIGHT)
            def _():
                p_copies[k].start()

        mask = rows < counts[i]
        attend(st, kv.at[i], {0: mask, 1: mask})

    q_copies[1].wait_recv()
    q_copies[2].wait_recv()

    targets = ((0, 1, partner), (1, 0, node(*own_side_near)), (1, 1, node(*side_far)))
    o_copies = {}

    def give(n):
        st, mi, to = targets[n]
        for g in range(2):
            for u in range(2):
                c = (g * 2 + mi) * 2 + u
                share = l_ref[st, c:c + 1, :]
                o_out[g, n, u] = (acc[st, c] * (1.0 / share)).astype(jnp.bfloat16)
                st_out[g, n, u:u + 1, :] = m_ref[st, c:c + 1, :]
                st_out[g, n, 2 + u:3 + u, :] = share
            e = g * 3 + n
            pair = (
                remote(st_out.at[g, n], st_in.at[g, n], t_send.at[e], t_recv.at[e], to),
                remote(o_out.at[g, n], o_in.at[g, n], o_send.at[e], o_recv.at[e], to),
            )
            for copy in pair:
                copy.start()
            o_copies[g, n] = pair

    def side_unit(i, carry):
        unit(1, i)
        return carry

    def home_unit(i, carry):
        unit(0, i)
        return carry

    lax.fori_loop(SELF[1], SIDE_END, side_unit, 0)
    give(2)
    give(1)
    lax.fori_loop(SIDE_END, PAGES, home_unit, 0)
    give(0)

    a_copies = {}
    live = lax.broadcasted_iota(jnp.int32, (1, ROWS), 1) < here
    for g in range(2):
        for n in range(3):
            for copy in o_copies[g, n]:
                copy.wait_recv()
        for u in range(2):
            c = g * 4 + u
            tops = [m_ref[0, c:c + 1, :]] + [st_in[g, n, u:u + 1, :] for n in range(3)]
            sums = [l_ref[0, c:c + 1, :]] + [st_in[g, n, 2 + u:3 + u, :] for n in range(3)]
            top = jnp.maximum(jnp.maximum(tops[0], tops[1]), jnp.maximum(tops[2], tops[3]))
            factors = [jnp.exp2((t - top) * SCALE2) for t in tops]
            shares = [f * l for f, l in zip(factors, sums)]
            whole = shares[0] + shares[1] + shares[2] + shares[3]
            inverse = jnp.where(live, 1.0 / whole, 0.0)
            value = acc[0, c] * (factors[0] * inverse)
            for n in range(3):
                value += o_in[g, n, u].astype(jnp.float32) * (shares[n + 1] * inverse)
            first = (2 * g + u) * HEAD_WIDTH
            attn[y, :, first:first + HEAD_WIDTH] = value.T.astype(jnp.bfloat16)
        half = pl.ds(g * 256, 256)
        for dy in (2, 1, 3):
            e = g * 3 + dy - 1
            copy = remote(
                attn.at[y, :, half], attn.at[y, :, half], a_send.at[e], a_recv.at[e], chip(dy)
            )
            copy.start()
            a_copies[g, dy] = copy

    own_weight.wait()
    total[...] = jnp.dot(attn[y], w_all[y], preferred_element_type=jnp.float32)
    for n, dy in enumerate((1, 3, 2)):
        w_copies[n].wait_recv()
    for g in range(2):
        for dy in (1, 3, 2):
            a_copies[g, dy].wait_recv()
            of = wrap(y - dy, NY)
            total[...] += jnp.dot(
                attn[of, :, g * 256:(g + 1) * 256], w_all[of, g * 256:(g + 1) * 256, :],
                preferred_element_type=jnp.float32,
            )

    turned[...] = total[...].T

    def columns_of(c):
        first = 64 * lax.rem(y, 2) + DEV_COLS * c
        return turned[pl.ds(pl.multiple_of(first, 32), DEV_COLS), :]

    sib_out[...] = columns_of(1 - core).astype(jnp.bfloat16)
    swap = remote(sib_out, sib_in, b_send.at[0], b_recv.at[0], sibling)
    swap.start()
    own = columns_of(core)
    swap.wait_recv()
    out_ref[...] = (own + sib_in[...].astype(jnp.float32)).astype(jnp.bfloat16)

    for copy in q_copies + w_copies + p_copies[2:] + list(a_copies.values()) + [swap]:
        copy.wait_send()
    for pair in o_copies.values():
        for copy in pair:
            copy.wait_send()


def shards(queries, suffix_key_value, pooled_pages, out_weight, page_table, prefix_len, suffix_len):
    vmem = pltpu.VMEM
    dma = pltpu.SemaphoreType.DMA
    bf16, f32 = jnp.bfloat16, jnp.float32
    return pl.pallas_call(
        kernel,
        out_shape=jax.ShapeDtypeStruct((DEV_COLS, ROWS), bf16),
        in_specs=[pl.BlockSpec(memory_space=vmem)]
        + [pl.BlockSpec(memory_space=pltpu.SMEM)] * 2
        + [pl.BlockSpec(memory_space=pl.ANY)] * 4,
        out_specs=pl.BlockSpec(memory_space=vmem),
        scratch_shapes=[
            vmem((PAGES, ROWS, 2, 256), bf16),
            vmem((PAGES, 2, ROWS, 256), bf16),
            vmem((PAGES + 1, 2, ROWS, 256), bf16),
            vmem((ROWS, 2, 256), bf16),
            vmem((2, 2, ROWS, 512), bf16),
            vmem((NY, 512, WIDE), bf16),
            vmem((2, 8, HEAD_WIDTH, ROWS), f32),
            vmem((2, 8, ROWS), f32),
            vmem((2, 8, ROWS), f32),
            vmem((2, 3, 2, HEAD_WIDTH, ROWS), bf16),
            vmem((2, 3, 2, HEAD_WIDTH, ROWS), bf16),
            vmem((2, 3, 8, ROWS), f32),
            vmem((2, 3, 8, ROWS), f32),
            vmem((NY, ROWS, 512), bf16),
            vmem((ROWS, WIDE), f32),
            vmem((WIDE, ROWS), f32),
            vmem((DEV_COLS, ROWS), bf16),
            vmem((DEV_COLS, ROWS), bf16),
            pltpu.SMEM((PAGES,), jnp.int32),
            pltpu.SMEM((PAGES,), jnp.int32),
            dma((4,)), dma((3,)), dma((3,)), dma((PAGES,)), dma((PAGES,)), dma((3,)), dma((3,)),
            dma((6,)), dma((6,)), dma((6,)), dma((6,)), dma((6,)), dma((6,)), dma((1,)), dma((1,)),
        ],
        compiler_params=pltpu.CompilerParams(
            collective_id=0, has_side_effects=True, vmem_limit_bytes=56 * 1024 * 1024
        ),
        name="paged_prefill",
    )(
        page_table, prefix_len, suffix_len, queries, suffix_key_value, pooled_pages, out_weight
    ).T


def solution(mesh):
    placed = (
        P("seq", "head"),
        P("seq", None, "head"),
        P("seq", None, None, "head"),
        P("head", None),
        P(),
        P(),
        P(),
    )
    return jax.shard_map(
        shards, mesh=mesh, in_specs=placed, out_specs=P("seq", "head"), check_vma=False
    )
```

```python
import functools

import jax
import jax.numpy as jnp
from jax import lax
from jax.experimental import pallas as pl
from jax.experimental.pallas import tpu as pltpu
from jax.sharding import PartitionSpec as P

D = 5376
QUERY_HEADS = 32
KEY_VALUE_HEADS = 16
HEAD_WIDTH = 128
NX, NZ, NY = 4, 8, 4
ROWS = 256
PAGES = 16
NEG = -1e30
SCALE2 = float(D // QUERY_HEADS) ** (-0.5) * 1.4426950408889634
CHIP_COLS = D // NY
WIDE = 1408
DEV_COLS = D // 8
MESH = pl.DeviceIdType.MESH

MESSAGES = (
    ("h", 0, 0),
    ("s", 0, 0),
    ("s", 0, 2),
    ("s", 1, 0),
    ("s", 3, 0),
    ("s", 0, 1),
    ("s", 2, 0),
    ("s", 1, 1),
    ("s", 3, 1),
    ("s", 3, 2),
    ("s", 2, 1),
    ("h", 0, 1),
    ("h", 0, -1),
    ("h", 1, 0),
    ("h", 1, 1),
    ("h", 1, -1),
)
SELF = (0, 1)
SIDE_END = 11
FLIGHT = 12
EARLY = 3


def sign(x, z):
    return 1 - 2 * lax.rem(x // 2 + z, 2)


def wrap(v, n):
    return lax.rem(v + 4 * n, n)


def home_step(j, dz):
    if j == 0:
        return 0, -dz
    return (-1, 0) if dz == 0 else (1, -dz)


def dest_of(message, x, z):
    kind, a, b = message
    if kind == "h":
        dx, dz = home_step(a, b)
        return wrap(x + dx, NX), wrap(z + dz, NZ)
    to = wrap(x + a, NX)
    return to, wrap(z - sign(to, z + b) * b, NZ)


def source_of(message, x, z):
    kind, a, b = message
    if kind == "h":
        dx, dz = home_step(a, b)
        return wrap(x - dx, NX), wrap(z - dz, NZ)
    return wrap(x - a, NX), wrap(z + sign(x, z) * b, NZ)


def request_of(message, x, z):
    if message[0] == "h":
        return lax.rem(x, 2) * NZ + z
    return lax.rem(x, 2) * NZ + wrap(z - 2 * sign(x, z), NZ)


def kernel(
    owners, prefix_len, suffix_len, q_hbm, skv_hbm, pages_hbm, w_hbm, out_ref,
    pages, sending, kv, skv, q_all, w_all, acc, m_ref, l_ref,
    o_out, o_in, st_out, st_in, attn, total, turned, sib_out, sib_in, slots, counts,
    local_sem, q_send, q_recv, p_send, p_recv, w_send, w_recv,
    o_send, o_recv, t_send, t_recv, a_send, a_recv, b_send, b_recv,
):
    seq = lax.axis_index("seq")
    head = lax.axis_index("head")
    x, z = seq // NZ, lax.rem(seq, NZ)
    y, core = head // 2, lax.rem(head, 2)
    s = sign(x, z)

    def node(xx, zz):
        return {"seq": xx * NZ + zz, "head": head}

    def chip(dy):
        return {"seq": seq, "head": wrap(y + dy, NY) * 2 + core}

    sibling = {"seq": seq, "head": y * 2 + 1 - core}
    partner = node(wrap(x + 2, NX), z)
    side_near = (x, wrap(z + 2 * s, NZ))
    side_far = (wrap(x + 2, NX), wrap(z - 2 * s, NZ))
    own_side_near = (x, wrap(z - 2 * s, NZ))

    local = [
        pltpu.make_async_copy(pages_hbm, pages, local_sem.at[0]),
        pltpu.make_async_copy(q_hbm, q_all.at[0, 0], local_sem.at[1]),
        pltpu.make_async_copy(skv_hbm, skv, local_sem.at[2]),
    ]
    for copy in local:
        copy.start()

    barrier = pltpu.get_barrier_semaphore()
    heard = 0
    for k, message in enumerate(MESSAGES):
        if k in SELF:
            continue
        pl.semaphore_signal(
            barrier, inc=1, device_id=node(*source_of(message, x, z)), device_id_type=MESH
        )
        heard += 1
    for where in (own_side_near, side_far):
        pl.semaphore_signal(barrier, inc=1, device_id=node(*where), device_id_type=MESH)
        heard += 1
    for dy in (1, 2, 3):
        pl.semaphore_signal(barrier, inc=1, device_id=chip(dy), device_id_type=MESH)
        heard += 1
    pl.semaphore_signal(barrier, inc=1, device_id=sibling, device_id_type=MESH)
    heard += 1

    acc[...] = jnp.zeros_like(acc)
    m_ref[...] = jnp.full(m_ref.shape, NEG, jnp.float32)
    l_ref[...] = jnp.zeros_like(l_ref)
    place = lax.broadcasted_iota(jnp.int32, (1, owners.shape[1]), 1) * ROWS
    for k, message in enumerate(MESSAGES):
        row = owners[pl.ds(request_of(message, *dest_of(message, x, z)), 1), :]
        slots[k] = jnp.sum(
            jnp.where(jnp.right_shift(row, 4) == seq, jnp.bitwise_and(row, PAGES - 1), 0)
        )
        served = request_of(message, x, z)
        xx, zz = source_of(message, x, z)
        row = owners[pl.ds(served, 1), :]
        counts[k] = jnp.sum(
            jnp.where(jnp.right_shift(row, 4) == xx * NZ + zz, prefix_len[served] - place, 0)
        )
    local[0].wait()

    def split(page, block):
        block[0] = page[:, 0, :]
        block[1] = page[:, 1, :].T

    def stage(first, last, buffer):
        def one(k, carry):
            split(pages[slots[k]], buffer.at[k])
            return carry

        lax.fori_loop(first, last, one, 0)

    stage(2, 6, sending)
    pl.semaphore_wait(barrier, heard)

    def remote(src, dst, send, recv, to):
        return pltpu.make_async_remote_copy(
            src_ref=src, dst_ref=dst, send_sem=send, recv_sem=recv,
            device_id=to, device_id_type=MESH,
        )

    q_copies = [
        remote(q_hbm, q_all.at[0, 1], q_send.at[0], q_recv.at[0], partner),
        remote(q_hbm, q_all.at[1, 0], q_send.at[1], q_recv.at[1], node(*side_near)),
        remote(q_hbm, q_all.at[1, 1], q_send.at[2], q_recv.at[2], node(*side_far)),
    ]
    for copy in q_copies:
        copy.start()

    def column(of):
        return pl.multiple_of(((21 * of) // 2) * 128, 128)

    own_weight = pltpu.make_async_copy(
        w_hbm.at[:, pl.ds(column(y), WIDE)], w_all.at[y], local_sem.at[3]
    )
    own_weight.start()
    w_copies = []
    for dy in (1, 3, 2):
        of = wrap(y + dy, NY)
        w_copies.append(
            remote(
                w_hbm.at[:, pl.ds(column(of), WIDE)], w_all.at[y],
                w_send.at[dy - 1], w_recv.at[dy - 1], chip(dy),
            )
        )
        w_copies[-1].start()

    p_copies = []
    for k, message in enumerate(MESSAGES):
        p_copies.append(
            remote(
                sending.at[k], kv.at[k], p_send.at[k], p_recv.at[k],
                node(*dest_of(message, x, z)),
            )
        )
    for k in range(2, 2 + EARLY):
        p_copies[k].start()
    stage(6, SIDE_END, sending)
    stage(SIDE_END, PAGES, sending)
    for k in range(2 + EARLY, 2 + FLIGHT):
        p_copies[k].start()

    rows = lax.broadcasted_iota(jnp.int32, (ROWS, ROWS), 0)
    cols = lax.broadcasted_iota(jnp.int32, (ROWS, ROWS), 1)

    def attend(st, block, masks, members=(0, 1)):
        for g in range(2):
            lanes = slice(g * HEAD_WIDTH, (g + 1) * HEAD_WIDTH)
            keys = block[0, :, lanes]
            values = block[1, lanes, :]
            parts = [(mi, u) for mi in members for u in range(2)]
            scores, olds = [], []
            for mi, u in parts:
                first = (2 * g + u) * HEAD_WIDTH
                raw = lax.dot_general(
                    keys, q_all[st, mi, :, first:first + HEAD_WIDTH],
                    (((1,), (1,)), ((), ())), preferred_element_type=jnp.float32,
                )
                scores.append(jnp.where(masks[mi], raw, NEG))
                c = (g * 2 + mi) * 2 + u
                olds.append((m_ref[st, c:c + 1, :], l_ref[st, c:c + 1, :]))
            results = []
            for score, (old, share) in zip(scores, olds):
                new = jnp.maximum(old, jnp.max(score, axis=0, keepdims=True))
                weights = jnp.exp2((score - new) * SCALE2)
                keep = jnp.exp2((old - new) * SCALE2)
                share = share * keep + jnp.sum(weights, axis=0, keepdims=True)
                mixed = jnp.dot(
                    values, weights.astype(jnp.bfloat16), preferred_element_type=jnp.float32
                )
                results.append((new, share, keep, mixed))
            for (mi, u), (new, share, keep, mixed) in zip(parts, results):
                c = (g * 2 + mi) * 2 + u
                m_ref[st, c:c + 1, :] = new
                l_ref[st, c:c + 1, :] = share
                acc[st, c] = acc[st, c] * keep + mixed

    member = x // 2
    mine = suffix_len[lax.rem(x, 2) * NZ + z]
    here = mine - member * ROWS
    stage(0, 2, kv)
    local[2].wait()
    split(skv[...], kv.at[PAGES])
    local[1].wait()
    own_mask = rows < counts[0]
    attend(0, kv.at[PAGES], {0: (rows <= cols) & (rows < here)}, (0,))
    attend(0, kv.at[0], {0: own_mask}, (0,))
    q_copies[0].wait_recv()
    attend(0, kv.at[PAGES], {1: rows < here * (1 - member)}, (1,))
    attend(0, kv.at[0], {1: own_mask}, (1,))
    def unit(st, i):
        @pl.when(i != SELF[1])
        def _():
            remote(
                sending.at[i], kv.at[i], p_send.at[i], p_recv.at[i], partner
            ).wait_recv()

        for k in range(2 + FLIGHT, PAGES):
            @pl.when(i == k - FLIGHT)
            def _():
                p_copies[k].start()

        mask = rows < counts[i]
        attend(st, kv.at[i], {0: mask, 1: mask})

    q_copies[1].wait_recv()
    q_copies[2].wait_recv()

    targets = ((0, 1, partner), (1, 0, node(*own_side_near)), (1, 1, node(*side_far)))
    o_copies = {}

    def give(n):
        st, mi, to = targets[n]
        for g in range(2):
            for u in range(2):
                c = (g * 2 + mi) * 2 + u
                share = l_ref[st, c:c + 1, :]
                o_out[g, n, u] = (acc[st, c] * (1.0 / share)).astype(jnp.bfloat16)
                st_out[g, n, u:u + 1, :] = m_ref[st, c:c + 1, :]
                st_out[g, n, 2 + u:3 + u, :] = share
            e = g * 3 + n
            pair = (
                remote(st_out.at[g, n], st_in.at[g, n], t_send.at[e], t_recv.at[e], to),
                remote(o_out.at[g, n], o_in.at[g, n], o_send.at[e], o_recv.at[e], to),
            )
            for copy in pair:
                copy.start()
            o_copies[g, n] = pair

    def side_unit(i, carry):
        unit(1, i)
        return carry

    def home_unit(i, carry):
        unit(0, i)
        return carry

    lax.fori_loop(SELF[1], SIDE_END, side_unit, 0)
    give(2)
    give(1)
    lax.fori_loop(SIDE_END, PAGES, home_unit, 0)
    give(0)

    a_copies = {}
    live = lax.broadcasted_iota(jnp.int32, (1, ROWS), 1) < here
    for g in range(2):
        for n in range(3):
            for copy in o_copies[g, n]:
                copy.wait_recv()
        for u in range(2):
            c = g * 4 + u
            tops = [m_ref[0, c:c + 1, :]] + [st_in[g, n, u:u + 1, :] for n in range(3)]
            sums = [l_ref[0, c:c + 1, :]] + [st_in[g, n, 2 + u:3 + u, :] for n in range(3)]
            top = jnp.maximum(jnp.maximum(tops[0], tops[1]), jnp.maximum(tops[2], tops[3]))
            factors = [jnp.exp2((t - top) * SCALE2) for t in tops]
            shares = [f * l for f, l in zip(factors, sums)]
            whole = shares[0] + shares[1] + shares[2] + shares[3]
            inverse = jnp.where(live, 1.0 / whole, 0.0)
            value = acc[0, c] * (factors[0] * inverse)
            for n in range(3):
                value += o_in[g, n, u].astype(jnp.float32) * (shares[n + 1] * inverse)
            first = (2 * g + u) * HEAD_WIDTH
            attn[y, :, first:first + HEAD_WIDTH] = value.T.astype(jnp.bfloat16)
        half = pl.ds(g * 256, 256)
        for dy in (2, 1, 3):
            e = g * 3 + dy - 1
            copy = remote(
                attn.at[y, :, half], attn.at[y, :, half], a_send.at[e], a_recv.at[e], chip(dy)
            )
            copy.start()
            a_copies[g, dy] = copy

    own_weight.wait()
    total[...] = jnp.dot(attn[y], w_all[y], preferred_element_type=jnp.float32)
    for n, dy in enumerate((1, 3, 2)):
        w_copies[n].wait_recv()
    for g in range(2):
        for dy in (1, 3, 2):
            a_copies[g, dy].wait_recv()
            of = wrap(y - dy, NY)
            total[...] += jnp.dot(
                attn[of, :, g * 256:(g + 1) * 256], w_all[of, g * 256:(g + 1) * 256, :],
                preferred_element_type=jnp.float32,
            )

    turned[...] = total[...].T

    def columns_of(c):
        first = 64 * lax.rem(y, 2) + DEV_COLS * c
        return turned[pl.ds(pl.multiple_of(first, 32), DEV_COLS), :]

    sib_out[...] = columns_of(1 - core).astype(jnp.bfloat16)
    swap = remote(sib_out, sib_in, b_send.at[0], b_recv.at[0], sibling)
    swap.start()
    own = columns_of(core)
    swap.wait_recv()
    out_ref[...] = (own + sib_in[...].astype(jnp.float32)).astype(jnp.bfloat16)

    for copy in q_copies + w_copies + p_copies[2:] + list(a_copies.values()) + [swap]:
        copy.wait_send()
    for pair in o_copies.values():
        for copy in pair:
            copy.wait_send()


def shards(queries, suffix_key_value, pooled_pages, out_weight, page_table, prefix_len, suffix_len):
    vmem = pltpu.VMEM
    dma = pltpu.SemaphoreType.DMA
    bf16, f32 = jnp.bfloat16, jnp.float32
    return pl.pallas_call(
        kernel,
        out_shape=jax.ShapeDtypeStruct((DEV_COLS, ROWS), bf16),
        in_specs=[pl.BlockSpec(memory_space=vmem)]
        + [pl.BlockSpec(memory_space=pltpu.SMEM)] * 2
        + [pl.BlockSpec(memory_space=pl.ANY)] * 4,
        out_specs=pl.BlockSpec(memory_space=vmem),
        scratch_shapes=[
            vmem((PAGES, ROWS, 2, 256), bf16),
            vmem((PAGES, 2, ROWS, 256), bf16),
            vmem((PAGES + 1, 2, ROWS, 256), bf16),
            vmem((ROWS, 2, 256), bf16),
            vmem((2, 2, ROWS, 512), bf16),
            vmem((NY, 512, WIDE), bf16),
            vmem((2, 8, HEAD_WIDTH, ROWS), f32),
            vmem((2, 8, ROWS), f32),
            vmem((2, 8, ROWS), f32),
            vmem((2, 3, 2, HEAD_WIDTH, ROWS), bf16),
            vmem((2, 3, 2, HEAD_WIDTH, ROWS), bf16),
            vmem((2, 3, 8, ROWS), f32),
            vmem((2, 3, 8, ROWS), f32),
            vmem((NY, ROWS, 512), bf16),
            vmem((ROWS, WIDE), f32),
            vmem((WIDE, ROWS), f32),
            vmem((DEV_COLS, ROWS), bf16),
            vmem((DEV_COLS, ROWS), bf16),
            pltpu.SMEM((PAGES,), jnp.int32),
            pltpu.SMEM((PAGES,), jnp.int32),
            dma((4,)), dma((3,)), dma((3,)), dma((PAGES,)), dma((PAGES,)), dma((3,)), dma((3,)),
            dma((6,)), dma((6,)), dma((6,)), dma((6,)), dma((6,)), dma((6,)), dma((1,)), dma((1,)),
        ],
        compiler_params=pltpu.CompilerParams(
            collective_id=0, has_side_effects=True, vmem_limit_bytes=56 * 1024 * 1024
        ),
        name="paged_prefill",
    )(
        page_table, prefix_len, suffix_len, queries, suffix_key_value, pooled_pages, out_weight
    ).T


def solution(mesh):
    placed = (
        P("seq", "head"),
        P("seq", None, "head"),
        P("seq", None, None, "head"),
        P("head", None),
        P(),
        P(),
        P(),
    )
    return jax.shard_map(
        shards, mesh=mesh, in_specs=placed, out_specs=P("seq", "head"), check_vma=False
    )
```
